1024 devices in a mesh: gx: 8 (over z_lo, core), gy: 16 (over z_hi, x), gz: 8 (over y).
Axes of the slice: x: 4, y: 8, z: 16 (z_hi: 4, z_lo: 4; z = z_hi * 4 + z_lo), core: 2. Of those that a mesh axis runs over, the one named last changes fastest.
Arguments:
- deflation: bfloat16 [64, 64, 32, 3, 128], P('gx', 'gy', 'gz'), may hold values from -0.33 to 0.33
- material: int32 [64, 64, 32], P('gx', 'gy', 'gz'), may hold values from 0 to 15
- moduli: float32 [16], replicated, may hold values from 1 to 100
- stencil: float32 [27, 3, 3], replicated, may hold values from -0.6 to 0.6
Outputs:
- coarse: float32 [8, 16, 128, 8, 27, 128], P('gx', 'gy', 'gz')
The draws below stay inside these ranges and needn't reach their ends.
All inputs are finite; a program needn't handle non-finite values.
Results may differ from the reference program's by a relative error of at most 0.005.
Values may be sent and summed in bfloat16 or wider, within the bound.
A program may use at most 32 MiB of HBM per device.

```python
import math
import jax
import jax.numpy as jnp
from jax import lax

CX = 8
CY = 4
CZ = 4
VECS = 128
NCLASS = 16
NEIGH = 27
NX = 64
NY = 64
NZ = 32
N_GX = 8
N_GY = 16
N_GZ = 8


def draw_deflation(key, part):
    first = jax.random.fold_in(jax.random.fold_in(key, 11), 0)
    shape = (NX, NY, NZ, 3, VECS)
    place_x = jnp.arange(NX, dtype=jnp.int32) % CX
    place_y = jnp.arange(NY, dtype=jnp.int32) % CY
    place_z = jnp.arange(NZ, dtype=jnp.int32) % CZ
    rim_x = jnp.where((place_x == 0) | (place_x == CX - 1), 3.0, 1.0)
    rim_y = jnp.where((place_y == 0) | (place_y == CY - 1), 3.0, 1.0)
    rim_z = jnp.where((place_z == 0) | (place_z == CZ - 1), 3.0, 1.0)
    envelope = rim_x[:, None, None] * rim_y[None, :, None] * rim_z[None, None, :]
    base = jnp.clip(jax.random.normal(first, shape, jnp.float32), -6.0, 6.0)
    return (0.002 * envelope[:, :, :, None, None] * base).astype(jnp.bfloat16)


def place_ends(entries, key, low, largest):
    spot = [jax.random.randint(jax.random.fold_in(key, axis), (), 0, length) for axis, length in enumerate(entries.shape)]
    widest = entries.shape.index(max(entries.shape))
    neighbour = spot[:widest] + [(spot[widest] + 1) % entries.shape[widest]] + spot[widest + 1:]
    return entries.at[tuple(spot)].set(low).at[tuple(neighbour)].set(largest)


def noise(rng, shape, deviation, bound, held_as=jnp.bfloat16):
    array = deviation * jax.random.normal(rng, shape, jnp.float32)
    return jnp.clip(array, min=-bound, max=bound).astype(held_as)


def setup_inputs(seed: int = 0) -> dict:
    keys = jax.random.split(jax.random.key(seed), 5)
    deflation = draw_deflation(jax.random.fold_in(keys[4], 71), 0)
    material = place_ends(jax.random.randint(keys[1], (NX, NY, NZ), 0, NCLASS), jax.random.fold_in(keys[1], 1), 0, NCLASS - 1).astype(jnp.int32)
    moduli = jnp.clip(jnp.exp(jax.random.uniform(keys[2], (NCLASS,), jnp.float32, math.log(1.0), math.log(100.0))), 1.0, 100.0)
    stencil = noise(keys[3], (NEIGH, 3, 3), 0.111, 0.6, jnp.float32)
    return {"deflation": deflation, "material": material, "moduli": moduli, "stencil": stencil}


def offset_list():
    result = []
    for first in (-1, 0, 1):
        for second in (-1, 0, 1):
            for third in (-1, 0, 1):
                result.append((first, second, third))
    return result

def spread(own, stencil):
    len_x = own.shape[0] + 2
    len_y = own.shape[1] + 2
    len_z = own.shape[2] + 2
    padded = jnp.pad(own, ((2, 2), (2, 2), (2, 2), (0, 0), (0, 0))).astype(jnp.float32)
    coupling = stencil.astype(jnp.float32)
    totals = [jnp.zeros((len_x, len_y, len_z, own.shape[4]), jnp.float32) for _ in range(3)]
    for index, offset in enumerate(offset_list()):
        window = padded[1 - offset[0]:1 - offset[0] + len_x, 1 - offset[1]:1 - offset[1] + len_y, 1 - offset[2]:1 - offset[2] + len_z]
        for source in range(3):
            plane = window[:, :, :, source, :]
            for target in range(3):
                totals[target] = totals[target] + coupling[index, source, target] * plane
    return jnp.stack(totals, axis=3)

def region(field, offset):
    pieces = field
    for axis in range(3):
        length = field.shape[axis]
        if offset[axis] < 0:
            start, extent = (0, 1)
        elif offset[axis] == 0:
            start, extent = (1, length - 2)
        else:
            start, extent = (length - 1, 1)
        pieces = lax.slice_in_dim(pieces, start, start + extent, axis=axis)
    return pieces.reshape(-1, pieces.shape[-1])

def contract(left, right):
    return lax.dot_general(left, right, (((0,), (0,)), ((), ())), preferred_element_type=jnp.float32)

def subdomain_blocks(cycle, stencil):
    own = cycle[1:-1, 1:-1, 1:-1]
    image = spread(own, stencil).astype(jnp.bfloat16)
    return jnp.stack([contract(region(image, offset), region(cycle, offset)) for offset in offset_list()])

def reference(deflation, material, moduli, stencil):
    root = jnp.sqrt(moduli)
    cell_roots = root[material]
    padded_vectors = jnp.pad(deflation, ((1, 1), (1, 1), (1, 1), (0, 0), (0, 0)))
    padded_roots = jnp.pad(cell_roots, 1)
    count = N_GX * N_GY * N_GZ

    def single(index):
        first = index // (N_GY * N_GZ)
        second = index // N_GZ % N_GY
        third = index % N_GZ
        block = lax.dynamic_slice(padded_vectors, (first * CX, second * CY, third * CZ, jnp.int32(0), jnp.int32(0)), (CX + 2, CY + 2, CZ + 2, 3, VECS))
        scales = lax.dynamic_slice(padded_roots, (first * CX, second * CY, third * CZ), (CX + 2, CY + 2, CZ + 2))
        cycle = (block.astype(jnp.float32) * scales[:, :, :, None, None]).astype(jnp.bfloat16)
        return subdomain_blocks(cycle, stencil)
    blocks = lax.map(single, jnp.arange(count, dtype=jnp.int32))
    blocks = blocks.reshape(N_GX, N_GY, N_GZ, NEIGH, VECS, VECS)
    return jnp.transpose(blocks, (0, 1, 4, 2, 3, 5))
```

```python
import functools

import jax
import jax.numpy as jnp
import numpy as np
from jax import lax
from jax.experimental import pallas as pl
from jax.experimental.pallas import tpu as pltpu
from jax.sharding import PartitionSpec as P

MESH = pl.DeviceIdType.MESH
HIGHEST = lax.Precision.HIGHEST
CX, CY, CZ, VECS = 8, 4, 4, 128
PLANE = CY * 3 * CZ
OFFSETS = [(i, j, k) for i in (-1, 0, 1) for j in (-1, 0, 1) for k in (-1, 0, 1)]
NEIGHBOURS = [o for o in OFFSETS if o != (0, 0, 0)]
GROUPS = (
    [(0, 0, 0)],
    [o for o in NEIGHBOURS if o[1] == 0],
    [o for o in NEIGHBOURS if o[1] != 0],
)
ORDER = [o for g in GROUPS for o in g]
STARTS = [sum(len(g) for g in GROUPS[:i]) for i in range(len(GROUPS))]


def number(o):
    return 9 * (o[0] + 1) + 3 * (o[1] + 1) + o[2] + 1


def side(v):
    return 1 if v > 0 else 0


def pair(v, w):
    return 2 * side(v) + side(w)


def image_rows():
    rows = [(y, z, b) for y in range(CY) for b in range(3) for z in range(CZ)]
    for y in (-1, CY):
        rows += [(y, z, b) for b in range(3) for z in range(CZ)] + [None] * 4
    for z in (-1, CZ):
        rows += [(y, z, b) for y in range(CY) for b in range(3)] + [None] * 4
    for y in (-1, CY):
        for z in (-1, CZ):
            rows += [(y, z, b) for b in range(3)] + [None]
    return rows


@functools.cache
def tables():
    rows = image_rows()
    index = np.full((128, 3 * PLANE), -1, np.int32)
    for r, row in enumerate(rows):
        if row is None:
            continue
        for p in range(3):
            for y in range(CY):
                for a in range(3):
                    for z in range(CZ):
                        oy, oz = row[0] - y, row[1] - z
                        if abs(oy) <= 1 and abs(oz) <= 1:
                            index[r, p * PLANE + y * 12 + a * 4 + z] = (3 * (oy + 1) + oz + 1) * 3 + row[2]
    widen = np.zeros((3, 27, 3 * PLANE), np.float32)
    for b in range(3):
        for p in range(3):
            for y in range(CY):
                for a in range(3):
                    for z in range(CZ):
                        widen[b, (2 - p) * 9 + a * 3 + b, p * PLANE + y * 12 + a * 4 + z] = 1
    pack = np.zeros((80, PLANE), np.float32)
    for r, row in enumerate(rows[48:]):
        if row is not None:
            y, z, a = row
            pack[r, (y % CY) * 12 + a * 4 + z % CZ] = 1
    regroup = np.zeros((128, 128), np.float32)
    for j in range(4):
        for x in range(CX):
            for b in range(4):
                regroup[j * 32 + x * 4 + b, x * 16 + j * 4 + b] = 1
    place = np.zeros((PLANE, 16), np.float32)
    for y in range(CY):
        for a in range(3):
            for z in range(CZ):
                place[y * 12 + a * 4 + z, y * CZ + z] = 1
    return index, widen, pack, regroup, place


def dot(a, b, precision=None):
    return jnp.dot(a, b, preferred_element_type=jnp.float32, precision=precision)


def contract(left, right):
    return lax.dot_general(left, right, (((0,), (0,)), ((), ())), preferred_element_type=jnp.float32)


def kernel(
    sizes,
    vec_ref, mat_ref, mod_ref, sten_ref, index_ref, widen_ref, pack_ref, regroup_ref, place_ref,
    out_ref,
    xp, pk, edge, cor, hx, hy, hz, hyz, hxy, hxz, hc, ic, iyz, icn, ie, stage, recv,
    halo_send, halo_recv, row_send, row_recv,
):
    n_x, n_y, n_z = sizes
    rows = VECS // n_z
    me = (lax.axis_index("gx"), lax.axis_index("gy"), lax.axis_index("gz"))

    def at(o):
        return tuple(lax.rem(me[i] + (o[i] + sizes[i]), sizes[i]) for i in range(3))

    line = [d for d in range(1, n_z) if d not in (1, n_z - 1)]
    barrier = pltpu.get_barrier_semaphore()
    for o in NEIGHBOURS:
        pl.semaphore_signal(barrier, inc=1, device_id=at(o), device_id_type=MESH)
    for d in line:
        pl.semaphore_signal(barrier, inc=1, device_id=at((0, 0, d)), device_id_type=MESH)

    mat = mat_ref[...]
    value = jnp.zeros(mat.shape, jnp.float32)
    for c in range(16):
        value = jnp.where(mat == c, mod_ref[c], value)
    root = jnp.sqrt(value)
    wide = jnp.concatenate([jnp.broadcast_to(root[:, x : x + 1], (16, VECS)) for x in range(CX)], axis=1)
    scale = dot(place_ref[...], wide, HIGHEST)
    empty = jnp.zeros((PLANE, VECS), jnp.bfloat16)
    for i in (0, 1, CX + 2, CX + 3):
        xp[i] = empty
    class_of = lax.broadcasted_iota(jnp.int32, (16, VECS), 0) // 4
    for x in range(CX):
        plane = (vec_ref[x].astype(jnp.float32) * scale[:, x * VECS : (x + 1) * VECS]).astype(jnp.bfloat16)
        xp[2 + x] = plane
        packed = dot(pack_ref[...], plane)
        for k in range(5):
            pk[k, x] = packed[16 * k : 16 * k + 16].astype(jnp.bfloat16)
        if x in (0, CX - 1):
            first = 0 if x == CX - 1 else 4
            for j in range(4):
                cor[first + j] = jnp.where(class_of == j, packed[64:80], 0.0).astype(jnp.bfloat16)
    dense = dot(regroup_ref[...], pk[4].reshape(CX * 16, VECS)).astype(jnp.bfloat16)
    for j in range(4):
        edge[j] = dense[32 * j : 32 * j + 32]

    pl.semaphore_wait(barrier, len(NEIGHBOURS) + len(line))

    def halo(r):
        xi = CX - 1 if r[0] < 0 else 0
        if r[1] == 0 and r[2] == 0:
            return xp.at[2 + xi], hx.at[side(r[0])]
        if r[0] == 0 and r[2] == 0:
            return pk.at[side(r[1])], hy.at[side(r[1])]
        if r[0] == 0 and r[1] == 0:
            return pk.at[2 + side(r[2])], hz.at[side(r[2])]
        if r[0] == 0:
            return edge.at[pair(r[1], r[2])], hyz.at[pair(r[1], r[2])]
        if r[2] == 0:
            return pk.at[side(r[1]), xi], hxy.at[pair(r[0], r[1])]
        if r[1] == 0:
            return pk.at[2 + side(r[2]), xi], hxz.at[pair(r[0], r[2])]
        k = 4 * side(r[0]) + pair(r[1], r[2])
        return cor.at[k], hc.at[k]

    copies = {}
    for r in sorted(NEIGHBOURS, key=lambda r: (r[1] == 0, -abs(r[0]) - abs(r[2]))):
        src, dst = halo(r)
        k = NEIGHBOURS.index(r)
        copies[r] = pltpu.make_async_remote_copy(
            src_ref=src, dst_ref=dst, send_sem=halo_send.at[k], recv_sem=halo_recv.at[k],
            device_id=at((-r[0], -r[1], -r[2])), device_id_type=MESH,
        )
        copies[r].start()

    index = index_ref[...]
    matrix = jnp.zeros(index.shape, jnp.float32)
    for b in range(3):
        table = dot(sten_ref[...], widen_ref[b], HIGHEST)
        for km in range(9):
            matrix = jnp.where(index == km * 3 + b, table[km : km + 1, :], matrix)
    high = matrix.astype(jnp.bfloat16)
    low = (matrix - high.astype(jnp.float32)).astype(jnp.bfloat16)
    for i in range(CX + 2):
        window = xp[i : i + 3].reshape(3 * PLANE, VECS)
        image = (dot(high, window) + dot(low, window)).astype(jnp.bfloat16)
        ic[i] = image[0:48]
        for k in range(4):
            iyz[k, i] = image[48 + 16 * k : 64 + 16 * k]
        icn[i] = image[112:128]
    dense = dot(regroup_ref[...], icn[1 : CX + 1].reshape(CX * 16, VECS)).astype(jnp.bfloat16)
    for j in range(4):
        ie[j] = dense[32 * j : 32 * j + 32]

    def operands(o):
        xi = 0 if o[0] < 0 else CX + 1
        inner = slice(1, CX + 1)
        if o == (0, 0, 0):
            return ic[inner].reshape(CX * PLANE, VECS), xp[2 : CX + 2].reshape(CX * PLANE, VECS)
        if o[1] == 0 and o[2] == 0:
            return ic[xi], hx[side(o[0])]
        if o[0] == 0 and o[2] == 0:
            k = side(o[1])
            return iyz[k, inner].reshape(CX * 16, VECS), hy[k].reshape(CX * 16, VECS)
        if o[0] == 0 and o[1] == 0:
            k = side(o[2])
            return iyz[2 + k, inner].reshape(CX * 16, VECS), hz[k].reshape(CX * 16, VECS)
        if o[0] == 0:
            k = pair(o[1], o[2])
            return ie[k], hyz[k]
        if o[2] == 0:
            return iyz[side(o[1]), xi], hxy[pair(o[0], o[1])]
        if o[1] == 0:
            return iyz[2 + side(o[2]), xi], hxz[pair(o[0], o[2])]
        return icn[xi], hc[4 * side(o[0]) + pair(o[1], o[2])]

    def inside(o):
        ok = None
        for i in range(3):
            if o[i] == 0:
                continue
            here = me[i] > 0 if o[i] < 0 else me[i] < sizes[i] - 1
            ok = here if ok is None else jnp.logical_and(ok, here)
        return ok

    def rows_copy(g, d, target, source):
        slots = pl.ds(STARTS[g], len(GROUPS[g]))
        return pltpu.make_async_remote_copy(
            src_ref=stage.at[target, slots], dst_ref=recv.at[source, slots],
            send_sem=row_send.at[g, d - 1], recv_sem=row_recv.at[g, d - 1],
            device_id=(me[0], me[1], target), device_id_type=MESH,
        )

    distances = sorted(range(1, n_z), key=lambda d: -min(d, n_z - d))
    for g, group in enumerate(GROUPS):
        for o in group:
            if o in copies:
                copies[o].wait_recv()
        for k, o in enumerate(group):
            left, right = operands(o)
            block = contract(left, right)
            if o != (0, 0, 0):
                block = jnp.where(inside(o), block, 0.0)
            stage[:, STARTS[g] + k] = block.reshape(n_z, rows, VECS).astype(jnp.bfloat16)
        for d in distances:
            rows_copy(g, d, lax.rem(me[2] + d, n_z), me[2]).start()

    def put(source, values):
        for k, o in enumerate(ORDER):
            out_ref.at[source][pl.ds(number(o), rows, stride=32), :] = values(k).astype(jnp.float32)

    put(me[2], lambda k: stage[me[2], k])
    for r in NEIGHBOURS:
        copies[r].wait_send()
    for d in reversed(distances):
        source = lax.rem(me[2] + n_z - d, n_z)
        for g in range(len(GROUPS)):
            rows_copy(g, d, lax.rem(me[2] + d, n_z), source).wait_recv()
        put(source, lambda k: recv[source, k])
    for d in distances:
        for g in range(len(GROUPS)):
            rows_copy(g, d, lax.rem(me[2] + d, n_z), me[2]).wait_send()


def body(sizes, deflation, material, moduli, stencil):
    n_z = sizes[2]
    rows = VECS // n_z
    vectors = jnp.transpose(deflation, (0, 1, 3, 2, 4)).reshape(CX, PLANE, VECS)
    classes = jnp.transpose(material, (1, 2, 0)).reshape(CY * CZ, CX)
    coupling = jnp.transpose(stencil.reshape(3, 9, 9), (1, 0, 2)).reshape(9, 27)
    index, widen, pack, regroup, place = tables()
    vmem = pl.BlockSpec(memory_space=pltpu.VMEM)
    b16 = jnp.bfloat16
    out = pl.pallas_call(
        functools.partial(kernel, sizes),
        out_shape=jax.ShapeDtypeStruct((n_z, rows * 32, VECS), jnp.float32),
        in_specs=[vmem, vmem, pl.BlockSpec(memory_space=pltpu.SMEM)] + [vmem] * 6,
        out_specs=vmem,
        scratch_shapes=[
            pltpu.VMEM((CX + 4, PLANE, VECS), b16),
            pltpu.VMEM((5, CX, 16, VECS), b16),
            pltpu.VMEM((4, 32, VECS), b16),
            pltpu.VMEM((8, 16, VECS), b16),
            pltpu.VMEM((2, PLANE, VECS), b16),
            pltpu.VMEM((2, CX, 16, VECS), b16),
            pltpu.VMEM((2, CX, 16, VECS), b16),
            pltpu.VMEM((4, 32, VECS), b16),
            pltpu.VMEM((4, 16, VECS), b16),
            pltpu.VMEM((4, 16, VECS), b16),
            pltpu.VMEM((8, 16, VECS), b16),
            pltpu.VMEM((CX + 2, PLANE, VECS), b16),
            pltpu.VMEM((4, CX + 2, 16, VECS), b16),
            pltpu.VMEM((CX + 2, 16, VECS), b16),
            pltpu.VMEM((4, 32, VECS), b16),
            pltpu.VMEM((n_z, 27, rows, VECS), b16),
            pltpu.VMEM((n_z, 27, rows, VECS), b16),
            pltpu.SemaphoreType.DMA((26,)),
            pltpu.SemaphoreType.DMA((26,)),
            pltpu.SemaphoreType.DMA((len(GROUPS), n_z - 1)),
            pltpu.SemaphoreType.DMA((len(GROUPS), n_z - 1)),
        ],
        compiler_params=pltpu.CompilerParams(collective_id=0, has_side_effects=True),
        name="coarse",
    )(vectors, classes, moduli, coupling, index, widen, jnp.asarray(pack, b16), jnp.asarray(regroup, b16), place)
    result = out.reshape(n_z, rows, 32, VECS)[:, :, :27]
    return jnp.transpose(result, (1, 0, 2, 3)).reshape(1, 1, rows, n_z, 27, VECS)


def solution(mesh):
    sizes = tuple(mesh.shape[name] for name in ("gx", "gy", "gz"))
    in_specs = (P("gx", "gy", "gz", None, None), P("gx", "gy", "gz"), P(), P())
    out_specs = P("gx", "gy", "gz", None, None, None)
    return jax.shard_map(
        functools.partial(body, sizes), mesh=mesh, in_specs=in_specs, out_specs=out_specs, check_vma=False
    )
```

```python
import functools

import jax
import jax.numpy as jnp
import numpy as np
from jax import lax
from jax.experimental import pallas as pl
from jax.experimental.pallas import tpu as pltpu
from jax.sharding import PartitionSpec as P

MESH = pl.DeviceIdType.MESH
HIGHEST = lax.Precision.HIGHEST
CX, CY, CZ, VECS = 8, 4, 4, 128
PLANE = CY * 3 * CZ
OFFSETS = [(i, j, k) for i in (-1, 0, 1) for j in (-1, 0, 1) for k in (-1, 0, 1)]
NEIGHBOURS = [o for o in OFFSETS if o != (0, 0, 0)]
GROUPS = (
    [(0, 0, 0)],
    [o for o in NEIGHBOURS if o[1] == 0],
    [o for o in NEIGHBOURS if o[1] != 0],
)
ORDER = [o for g in GROUPS for o in g]
STARTS = [sum(len(g) for g in GROUPS[:i]) for i in range(len(GROUPS))]


def number(o):
    return 9 * (o[0] + 1) + 3 * (o[1] + 1) + o[2] + 1


def side(v):
    return 1 if v > 0 else 0


def pair(v, w):
    return 2 * side(v) + side(w)


def image_rows():
    rows = [(y, z, b) for y in range(CY) for b in range(3) for z in range(CZ)]
    for y in (-1, CY):
        rows += [(y, z, b) for b in range(3) for z in range(CZ)] + [None] * 4
    for z in (-1, CZ):
        rows += [(y, z, b) for y in range(CY) for b in range(3)] + [None] * 4
    for y in (-1, CY):
        for z in (-1, CZ):
            rows += [(y, z, b) for b in range(3)] + [None]
    return rows


@functools.cache
def tables():
    rows = image_rows()
    index = np.full((128, 3 * PLANE), -1, np.int32)
    for r, row in enumerate(rows):
        if row is None:
            continue
        for p in range(3):
            for y in range(CY):
                for a in range(3):
                    for z in range(CZ):
                        oy, oz = row[0] - y, row[1] - z
                        if abs(oy) <= 1 and abs(oz) <= 1:
                            index[r, p * PLANE + y * 12 + a * 4 + z] = (3 * (oy + 1) + oz + 1) * 3 + row[2]
    widen = np.zeros((3, 27, 3 * PLANE), np.float32)
    for n in range(27):
        for y in range(CY):
            for a in range(3):
                for z in range(CZ):
                    widen[a, n, (2 - n // 9) * PLANE + y * 12 + a * 4 + z] = 1
    chosen = (np.arange(27)[None, :] % 9 == np.arange(16)[:, None]).astype(np.float32)
    pack = np.zeros((80, PLANE), np.float32)
    for r, row in enumerate(rows[48:]):
        if row is not None:
            y, z, a = row
            pack[r, (y % CY) * 12 + a * 4 + z % CZ] = 1
    regroup = np.zeros((128, 128), np.float32)
    for j in range(4):
        for x in range(CX):
            for b in range(4):
                regroup[j * 32 + x * 4 + b, x * 16 + j * 4 + b] = 1
    place = np.zeros((PLANE, 16), np.float32)
    for y in range(CY):
        for a in range(3):
            for z in range(CZ):
                place[y * 12 + a * 4 + z, y * CZ + z] = 1
    return index, widen, chosen, pack, regroup, place


def dot(a, b, precision=None):
    return jnp.dot(a, b, preferred_element_type=jnp.float32, precision=precision)


def contract(left, right):
    return lax.dot_general(left, right, (((0,), (0,)), ((), ())), preferred_element_type=jnp.float32)


def kernel(
    sizes,
    vec_in, mat_in, mod_in, sten_in, index_in, widen_in, chosen_in, pack_in, regroup_in, place_in,
    out_ref,
    vec_ref, mat_ref, mod_ref, sten_ref, index_ref, widen_ref, chosen_ref, pack_ref, regroup_ref, place_ref, load_sem,
    xp, pk, edge, cor, hx, hy, hz, hyz, hxy, hxz, hc, ic, iyz, icn, ie, stage, recv,
    halo_send, halo_recv, row_send, row_recv,
):
    loads = [
        pltpu.make_async_copy(src, dst, load_sem.at[k])
        for k, (src, dst) in enumerate([
            (mat_in, mat_ref), (mod_in, mod_ref), (place_in, place_ref), (vec_in, vec_ref), (pack_in, pack_ref),
            (regroup_in, regroup_ref), (sten_in, sten_ref), (index_in, index_ref), (widen_in, widen_ref), (chosen_in, chosen_ref),
        ])
    ]
    for copy in loads:
        copy.start()
    n_z = sizes[2]
    rows = VECS // n_z
    me = (lax.axis_index("gx"), lax.axis_index("gy"), lax.axis_index("gz"))

    def at(o):
        return tuple(lax.rem(me[i] + (o[i] + sizes[i]), sizes[i]) for i in range(3))

    line = [d for d in range(1, n_z) if d not in (1, n_z - 1)]
    barrier = pltpu.get_barrier_semaphore()
    for o in NEIGHBOURS:
        pl.semaphore_signal(barrier, inc=1, device_id=at(o), device_id_type=MESH)
    for d in line:
        pl.semaphore_signal(barrier, inc=1, device_id=at((0, 0, d)), device_id_type=MESH)

    for copy in loads[:6]:
        copy.wait()
    mat = mat_ref[...]
    value = jnp.zeros(mat.shape, jnp.float32)
    for c in range(16):
        value = jnp.where(mat == c, mod_ref[c], value)
    root = jnp.sqrt(value)
    wide = jnp.concatenate([jnp.broadcast_to(root[:, x : x + 1], (16, VECS)) for x in range(CX)], axis=1)
    scale = dot(place_ref[...], wide, HIGHEST)
    empty = jnp.zeros((PLANE, VECS), jnp.bfloat16)
    for i in (0, 1, CX + 2, CX + 3):
        xp[i] = empty
    class_of = lax.broadcasted_iota(jnp.int32, (16, VECS), 0) // 4
    for x in range(CX):
        plane = (vec_ref[x].astype(jnp.float32) * scale[:, x * VECS : (x + 1) * VECS]).astype(jnp.bfloat16)
        xp[2 + x] = plane
        packed = dot(pack_ref[...], plane)
        for k in range(5):
            pk[k, x] = packed[16 * k : 16 * k + 16].astype(jnp.bfloat16)
        if x in (0, CX - 1):
            first = 0 if x == CX - 1 else 4
            for j in range(4):
                cor[first + j] = jnp.where(class_of == j, packed[64:80], 0.0).astype(jnp.bfloat16)
    dense = dot(regroup_ref[...], pk[4].reshape(CX * 16, VECS)).astype(jnp.bfloat16)
    for j in range(4):
        edge[j] = dense[32 * j : 32 * j + 32]

    pl.semaphore_wait(barrier, len(NEIGHBOURS) + len(line))

    def halo(r):
        xi = CX - 1 if r[0] < 0 else 0
        if r[1] == 0 and r[2] == 0:
            return xp.at[2 + xi], hx.at[side(r[0])]
        if r[0] == 0 and r[2] == 0:
            return pk.at[side(r[1])], hy.at[side(r[1])]
        if r[0] == 0 and r[1] == 0:
            return pk.at[2 + side(r[2])], hz.at[side(r[2])]
        if r[0] == 0:
            return edge.at[pair(r[1], r[2])], hyz.at[pair(r[1], r[2])]
        if r[2] == 0:
            return pk.at[side(r[1]), xi], hxy.at[pair(r[0], r[1])]
        if r[1] == 0:
            return pk.at[2 + side(r[2]), xi], hxz.at[pair(r[0], r[2])]
        k = 4 * side(r[0]) + pair(r[1], r[2])
        return cor.at[k], hc.at[k]

    copies = {}
    for r in sorted(NEIGHBOURS, key=lambda r: (r[1] == 0, -abs(r[0]) - abs(r[2]))):
        src, dst = halo(r)
        k = NEIGHBOURS.index(r)
        copies[r] = pltpu.make_async_remote_copy(
            src_ref=src, dst_ref=dst, send_sem=halo_send.at[k], recv_sem=halo_recv.at[k],
            device_id=at((-r[0], -r[1], -r[2])), device_id_type=MESH,
        )
        copies[r].start()

    for copy in loads[6:]:
        copy.wait()
    index = index_ref[...]
    matrix = jnp.zeros(index.shape, jnp.float32)
    chosen = chosen_ref[...]
    table = None
    for a in range(3):
        coupling = jnp.concatenate([chosen * sten_ref[a][b : b + 1, :] for b in range(3)], axis=0)
        term = dot(coupling, widen_ref[a], HIGHEST)
        table = term if table is None else table + term
    for b in range(3):
        for km in range(9):
            matrix = jnp.where(index == km * 3 + b, table[16 * b + km : 16 * b + km + 1, :], matrix)
    high = matrix.astype(jnp.bfloat16)
    low = (matrix - high.astype(jnp.float32)).astype(jnp.bfloat16)
    for i in range(CX + 2):
        window = xp[i : i + 3].reshape(3 * PLANE, VECS)
        image = (dot(high, window) + dot(low, window)).astype(jnp.bfloat16)
        ic[i] = image[0:48]
        for k in range(4):
            iyz[k, i] = image[48 + 16 * k : 64 + 16 * k]
        icn[i] = image[112:128]
    dense = dot(regroup_ref[...], icn[1 : CX + 1].reshape(CX * 16, VECS)).astype(jnp.bfloat16)
    for j in range(4):
        ie[j] = dense[32 * j : 32 * j + 32]

    def operands(o):
        xi = 0 if o[0] < 0 else CX + 1
        inner = slice(1, CX + 1)
        if o == (0, 0, 0):
            return ic[inner].reshape(CX * PLANE, VECS), xp[2 : CX + 2].reshape(CX * PLANE, VECS)
        if o[1] == 0 and o[2] == 0:
            return ic[xi], hx[side(o[0])]
        if o[0] == 0 and o[2] == 0:
            k = side(o[1])
            return iyz[k, inner].reshape(CX * 16, VECS), hy[k].reshape(CX * 16, VECS)
        if o[0] == 0 and o[1] == 0:
            k = side(o[2])
            return iyz[2 + k, inner].reshape(CX * 16, VECS), hz[k].reshape(CX * 16, VECS)
        if o[0] == 0:
            k = pair(o[1], o[2])
            return ie[k], hyz[k]
        if o[2] == 0:
            return iyz[side(o[1]), xi], hxy[pair(o[0], o[1])]
        if o[1] == 0:
            return iyz[2 + side(o[2]), xi], hxz[pair(o[0], o[2])]
        return icn[xi], hc[4 * side(o[0]) + pair(o[1], o[2])]

    def inside(o):
        ok = None
        for i in range(3):
            if o[i] == 0:
                continue
            here = me[i] > 0 if o[i] < 0 else me[i] < sizes[i] - 1
            ok = here if ok is None else jnp.logical_and(ok, here)
        return ok

    def rows_copy(g, d, target, source):
        slots = pl.ds(STARTS[g], len(GROUPS[g]))
        return pltpu.make_async_remote_copy(
            src_ref=stage.at[target, slots], dst_ref=recv.at[source, slots],
            send_sem=row_send.at[g, d - 1], recv_sem=row_recv.at[g, d - 1],
            device_id=(me[0], me[1], target), device_id_type=MESH,
        )

    distances = sorted(range(1, n_z), key=lambda d: -min(d, n_z - d))
    for g, group in enumerate(GROUPS):
        for o in group:
            if o in copies:
                copies[o].wait_recv()
        for k, o in enumerate(group):
            left, right = operands(o)
            block = contract(left, right)
            if o != (0, 0, 0):
                block = jnp.where(inside(o), block, 0.0)
            stage[:, STARTS[g] + k] = block.reshape(n_z, rows, VECS).astype(jnp.bfloat16)
        for d in distances:
            rows_copy(g, d, lax.rem(me[2] + d, n_z), me[2]).start()

    def put(source, values):
        for k, o in enumerate(ORDER):
            out_ref[pl.ds(number(o) * n_z + source, rows, stride=27 * n_z), :] = values(k).astype(jnp.float32)

    put(me[2], lambda k: stage[me[2], k])
    for r in NEIGHBOURS:
        copies[r].wait_send()
    for d in reversed(distances):
        source = lax.rem(me[2] + n_z - d, n_z)
        for g in range(len(GROUPS)):
            rows_copy(g, d, lax.rem(me[2] + d, n_z), source).wait_recv()
        put(source, lambda k: recv[source, k])
    for d in distances:
        for g in range(len(GROUPS)):
            rows_copy(g, d, lax.rem(me[2] + d, n_z), me[2]).wait_send()


def body(sizes, deflation, material, moduli, stencil):
    n_z = sizes[2]
    rows = VECS // n_z
    vectors = jnp.transpose(deflation, (0, 1, 3, 2, 4)).reshape(CX, PLANE, VECS)
    classes = jnp.transpose(material, (1, 2, 0)).reshape(CY * CZ, CX)
    coupling = jnp.transpose(stencil, (1, 2, 0))
    index, widen, chosen, pack, regroup, place = tables()
    b16 = jnp.bfloat16
    operands = (
        vectors, classes, moduli, coupling, index, widen, chosen,
        jnp.asarray(pack, b16), jnp.asarray(regroup, b16), place,
    )
    spaces = [pltpu.SMEM if k == 2 else pltpu.VMEM for k in range(len(operands))]
    out = pl.pallas_call(
        functools.partial(kernel, sizes),
        out_shape=jax.ShapeDtypeStruct((rows * 27 * n_z, VECS), jnp.float32),
        in_specs=[pl.BlockSpec(memory_space=pltpu.HBM)] * len(operands),
        out_specs=pl.BlockSpec(memory_space=pltpu.VMEM),
        scratch_shapes=[space(v.shape, v.dtype) for space, v in zip(spaces, operands)] + [
            pltpu.SemaphoreType.DMA((len(operands),)),
            pltpu.VMEM((CX + 4, PLANE, VECS), b16),
            pltpu.VMEM((5, CX, 16, VECS), b16),
            pltpu.VMEM((4, 32, VECS), b16),
            pltpu.VMEM((8, 16, VECS), b16),
            pltpu.VMEM((2, PLANE, VECS), b16),
            pltpu.VMEM((2, CX, 16, VECS), b16),
            pltpu.VMEM((2, CX, 16, VECS), b16),
            pltpu.VMEM((4, 32, VECS), b16),
            pltpu.VMEM((4, 16, VECS), b16),
            pltpu.VMEM((4, 16, VECS), b16),
            pltpu.VMEM((8, 16, VECS), b16),
            pltpu.VMEM((CX + 2, PLANE, VECS), b16),
            pltpu.VMEM((4, CX + 2, 16, VECS), b16),
            pltpu.VMEM((CX + 2, 16, VECS), b16),
            pltpu.VMEM((4, 32, VECS), b16),
            pltpu.VMEM((n_z, 27, rows, VECS), b16),
            pltpu.VMEM((n_z, 27, rows, VECS), b16),
            pltpu.SemaphoreType.DMA((26,)),
            pltpu.SemaphoreType.DMA((26,)),
            pltpu.SemaphoreType.DMA((len(GROUPS), n_z - 1)),
            pltpu.SemaphoreType.DMA((len(GROUPS), n_z - 1)),
        ],
        compiler_params=pltpu.CompilerParams(collective_id=0, has_side_effects=True, vmem_limit_bytes=24 * 2**20),
        name="coarse",
    )(*[pltpu.with_memory_space_constraint(v, pltpu.HBM) for v in operands])
    return jnp.transpose(out.reshape(1, 1, rows, 27, n_z, VECS), (0, 1, 2, 4, 3, 5))


def solution(mesh):
    sizes = tuple(mesh.shape[name] for name in ("gx", "gy", "gz"))
    in_specs = (P("gx", "gy", "gz", None, None), P("gx", "gy", "gz"), P(), P())
    out_specs = P("gx", "gy", "gz", None, None, None)
    return jax.shard_map(
        functools.partial(body, sizes), mesh=mesh, in_specs=in_specs, out_specs=out_specs, check_vma=False
    )
```

```python
import functools

import jax
import jax.numpy as jnp
import numpy as np
from jax import lax
from jax.experimental import pallas as pl
from jax.experimental.pallas import tpu as pltpu
from jax.sharding import PartitionSpec as P

MESH = pl.DeviceIdType.MESH
HIGHEST = lax.Precision.HIGHEST
CX, CY, CZ, VECS = 8, 4, 4, 128
PLANE = CY * 3 * CZ
OFFSETS = [(i, j, k) for i in (-1, 0, 1) for j in (-1, 0, 1) for k in (-1, 0, 1)]
CROSS = [(i, j) for i in (-1, 1) for j in (-1, 1)]
NEIGHBOURS = [o for o in OFFSETS if o != (0, 0, 0) and 0 in o]
GROUPS = (
    [(0, 0, 0)],
    [o for o in NEIGHBOURS if o[1] == 0],
    [o for o in NEIGHBOURS if o[0] == 0 and o[1] != 0],
)
ORDER = [o for g in GROUPS for o in g]
SLOTS = (slice(0, 2), slice(2, 10), slice(10, 16))
PLACES = [0] + list(range(2, 16))


def number(o):
    return 9 * (o[0] + 1) + 3 * (o[1] + 1) + o[2] + 1


def side(v):
    return 1 if v > 0 else 0


def pair(v, w):
    return 2 * side(v) + side(w)


def image_rows():
    rows = [(y, z, b) for y in range(CY) for b in range(3) for z in range(CZ)]
    for y in (-1, CY):
        rows += [(y, z, b) for b in range(3) for z in range(CZ)] + [None] * 4
    for z in (-1, CZ):
        rows += [(y, z, b) for y in range(CY) for b in range(3)] + [None] * 4
    for y in (-1, CY):
        for z in (-1, CZ):
            rows += [(y, z, b) for b in range(3)] + [None]
    return rows


@functools.cache
def tables():
    rows = image_rows()
    index = np.full((128, 3 * PLANE), -1, np.int32)
    for r, row in enumerate(rows):
        if row is None:
            continue
        for p in range(3):
            for y in range(CY):
                for a in range(3):
                    for z in range(CZ):
                        oy, oz = row[0] - y, row[1] - z
                        if abs(oy) <= 1 and abs(oz) <= 1:
                            index[r, p * PLANE + y * 12 + a * 4 + z] = (3 * (oy + 1) + oz + 1) * 3 + row[2]
    widen = np.zeros((3, 27, 3 * PLANE), np.float32)
    for n in range(27):
        for y in range(CY):
            for a in range(3):
                for z in range(CZ):
                    widen[a, n, (2 - n // 9) * PLANE + y * 12 + a * 4 + z] = 1
    chosen = (np.arange(27)[None, :] % 9 == np.arange(16)[:, None]).astype(np.float32)
    pack = np.zeros((80, PLANE), np.float32)
    for r, row in enumerate(rows[48:]):
        if row is not None:
            y, z, a = row
            pack[r, (y % CY) * 12 + a * 4 + z % CZ] = 1
    regroup = np.zeros((128, 128), np.float32)
    for j in range(4):
        for x in range(CX):
            for b in range(4):
                regroup[j * 32 + x * 4 + b, x * 16 + j * 4 + b] = 1
    place = np.zeros((PLANE, 16), np.float32)
    for y in range(CY):
        for a in range(3):
            for z in range(CZ):
                place[y * 12 + a * 4 + z, y * CZ + z] = 1
    choose = np.zeros((128, 12, 8, 16), np.float32)
    for g, (_, y) in enumerate(CROSS):
        for a in range(3):
            for z in range(CZ):
                choose[g * 32 + a * 4 + z, 3 * g + 1, :, a * 4 + z] = 1
            choose[g * 32 + 16 + pair(y, -1) * 4 + a, 3 * g, :, a * 4 + CZ - 1] = 1
            choose[g * 32 + 16 + pair(y, 1) * 4 + a, 3 * g + 2, :, a * 4] = 1
    return index, widen, chosen, pack, regroup, place, np.eye(128, dtype=np.float32), choose.reshape(128, 1536)


def dot(a, b, precision=None):
    return jnp.dot(a, b, preferred_element_type=jnp.float32, precision=precision)


def contract(left, right):
    return lax.dot_general(left, right, (((0,), (0,)), ((), ())), preferred_element_type=jnp.float32)


def kernel(
    sizes,
    vec_in, mat_in, mod_in, sten_in, index_in, widen_in, chosen_in, pack_in, regroup_in, place_in, eye_in, choose_in,
    out_ref,
    vec_ref, mat_ref, mod_ref, sten_ref, index_ref, widen_ref, chosen_ref, pack_ref, regroup_ref, place_ref, eye_ref, choose_ref, load_sem,
    xp, pk, edge, hx, hy, hz, hyz, hxy, hxz, ic, iyz, icn, ie, stage, recv, cells,
    halo_send, halo_recv, row_send, row_recv,
):
    loads = [
        pltpu.make_async_copy(src, dst, load_sem.at[k])
        for k, (src, dst) in enumerate([
            (mat_in, mat_ref), (mod_in, mod_ref), (place_in, place_ref), (vec_in, vec_ref), (pack_in, pack_ref),
            (regroup_in, regroup_ref), (sten_in, sten_ref), (index_in, index_ref), (widen_in, widen_ref), (chosen_in, chosen_ref),
            (eye_in, eye_ref), (choose_in, choose_ref),
        ])
    ]
    for copy in loads:
        copy.start()
    n_z = sizes[2]
    rows = VECS // n_z
    me = (lax.axis_index("gx"), lax.axis_index("gy"), lax.axis_index("gz"))

    def at(o):
        return tuple(lax.rem(me[i] + (o[i] + sizes[i]), sizes[i]) for i in range(3))

    line = [d for d in range(1, n_z) if d not in (1, n_z - 1)]
    barrier = pltpu.get_barrier_semaphore()
    for o in NEIGHBOURS:
        pl.semaphore_signal(barrier, inc=1, device_id=at(o), device_id_type=MESH)
    for d in line:
        pl.semaphore_signal(barrier, inc=1, device_id=at((0, 0, d)), device_id_type=MESH)

    for copy in loads[:6]:
        copy.wait()
    mat = mat_ref[...]
    value = jnp.zeros(mat.shape, jnp.float32)
    for c in range(16):
        value = jnp.where(mat == c, mod_ref[c], value)
    root = jnp.sqrt(value)
    wide = jnp.concatenate([jnp.broadcast_to(root[:, x : x + 1], (16, VECS)) for x in range(CX)], axis=1)
    scale = dot(place_ref[...], wide, HIGHEST)
    empty = jnp.zeros((PLANE, VECS), jnp.bfloat16)
    for i in (0, 1, CX + 2, CX + 3):
        xp[i] = empty
    for x in range(CX):
        plane = (vec_ref[x].astype(jnp.float32) * scale[:, x * VECS : (x + 1) * VECS]).astype(jnp.bfloat16)
        xp[2 + x] = plane
        packed = dot(pack_ref[...], plane)
        for k in range(5):
            pk[k, x] = packed[16 * k : 16 * k + 16].astype(jnp.bfloat16)
    dense = dot(regroup_ref[...], pk[4].reshape(CX * 16, VECS)).astype(jnp.bfloat16)
    for j in range(4):
        edge[j] = dense[32 * j : 32 * j + 32]

    pl.semaphore_wait(barrier, len(NEIGHBOURS) + len(line))

    def halo(r):
        xi = CX - 1 if r[0] < 0 else 0
        if r[1] == 0 and r[2] == 0:
            return xp.at[2 + xi], hx.at[side(r[0])]
        if r[0] == 0 and r[2] == 0:
            return pk.at[side(r[1])], hy.at[side(r[1])]
        if r[0] == 0 and r[1] == 0:
            return pk.at[2 + side(r[2])], hz.at[side(r[2])]
        if r[0] == 0:
            return edge.at[pair(r[1], r[2])], hyz.at[pair(r[1], r[2])]
        if r[2] == 0:
            return pk.at[side(r[1]), xi], hxy.at[pair(r[0], r[1])]
        return pk.at[2 + side(r[2]), xi], hxz.at[pair(r[0], r[2])]

    copies = {}
    for r in sorted(NEIGHBOURS, key=lambda r: (r[1] == 0, -abs(r[0]) - abs(r[2]))):
        src, dst = halo(r)
        k = NEIGHBOURS.index(r)
        copies[r] = pltpu.make_async_remote_copy(
            src_ref=src, dst_ref=dst, send_sem=halo_send.at[k], recv_sem=halo_recv.at[k],
            device_id=at((-r[0], -r[1], -r[2])), device_id_type=MESH,
        )
        copies[r].start()

    for copy in loads[6:]:
        copy.wait()
    index = index_ref[...]
    matrix = jnp.zeros(index.shape, jnp.float32)
    chosen = chosen_ref[...]
    table = None
    for a in range(3):
        coupling = jnp.concatenate([chosen * sten_ref[a][b : b + 1, :] for b in range(3)], axis=0)
        term = dot(coupling, widen_ref[a], HIGHEST)
        table = term if table is None else table + term
    for b in range(3):
        for km in range(9):
            matrix = jnp.where(index == km * 3 + b, table[16 * b + km : 16 * b + km + 1, :], matrix)
    high = matrix.astype(jnp.bfloat16)
    low = (matrix - high.astype(jnp.float32)).astype(jnp.bfloat16)
    for i in range(CX + 2):
        window = xp[i : i + 3].reshape(3 * PLANE, VECS)
        image = (dot(high, window) + dot(low, window)).astype(jnp.bfloat16)
        ic[i] = image[0:48]
        for k in range(4):
            iyz[k, i] = image[48 + 16 * k : 64 + 16 * k]
        icn[i] = image[112:128]
    dense = dot(regroup_ref[...], icn[1 : CX + 1].reshape(CX * 16, VECS)).astype(jnp.bfloat16)
    for j in range(4):
        ie[j] = dense[32 * j : 32 * j + 32]

    def operands(o):
        xi = 0 if o[0] < 0 else CX + 1
        inner = slice(1, CX + 1)
        if o == (0, 0, 0):
            return ic[inner].reshape(CX * PLANE, VECS), xp[2 : CX + 2].reshape(CX * PLANE, VECS)
        if o[1] == 0 and o[2] == 0:
            return ic[xi], hx[side(o[0])]
        if o[0] == 0 and o[2] == 0:
            k = side(o[1])
            return iyz[k, inner].reshape(CX * 16, VECS), hy[k].reshape(CX * 16, VECS)
        if o[0] == 0 and o[1] == 0:
            k = side(o[2])
            return iyz[2 + k, inner].reshape(CX * 16, VECS), hz[k].reshape(CX * 16, VECS)
        if o[0] == 0:
            k = pair(o[1], o[2])
            return ie[k], hyz[k]
        return iyz[2 + side(o[2]), xi], hxz[pair(o[0], o[2])]

    def inside(o):
        ok = None
        for i in range(3):
            if o[i] == 0:
                continue
            here = me[i] > 0 if o[i] < 0 else me[i] < sizes[i] - 1
            ok = here if ok is None else jnp.logical_and(ok, here)
        return ok

    def rows_copy(g, d, target, source):
        if g == len(GROUPS):
            src, dst = hxy, cells.at[source]
        else:
            slots = pl.ds(SLOTS[g].start, SLOTS[g].stop - SLOTS[g].start)
            src, dst = stage.at[target, slots], recv.at[source, slots]
        return pltpu.make_async_remote_copy(
            src_ref=src, dst_ref=dst, send_sem=row_send.at[g, d - 1], recv_sem=row_recv.at[g, d - 1],
            device_id=(me[0], me[1], target), device_id_type=MESH,
        )

    distances = sorted(range(1, n_z), key=lambda d: -min(d, n_z - d))

    def send(g):
        for d in distances:
            rows_copy(g, d, lax.rem(me[2] + d, n_z), me[2]).start()

    def receive(g, d):
        rows_copy(g, d, lax.rem(me[2] + d, n_z), lax.rem(me[2] + n_z - d, n_z)).wait_recv()

    few = [v for x, y in CROSS for v in (iyz[side(y), (CX + 1) * side(x)], icn[(CX + 1) * side(x)])]
    few = contract(jnp.concatenate(few, axis=0), eye_ref[...]).reshape(n_z, rows, VECS).astype(jnp.bfloat16)
    stage[:, 1] = few
    for g, group in enumerate(GROUPS):
        if g == 2:
            for x, y in CROSS:
                copies[x, y, 0].wait_recv()
            send(len(GROUPS))
            cells[me[2]] = hxy[...]
        for o in group:
            if o in copies:
                copies[o].wait_recv()
        for o in group:
            left, right = operands(o)
            block = contract(left, right)
            if o != (0, 0, 0):
                block = jnp.where(inside(o), block, 0.0)
            stage[:, PLACES[ORDER.index(o)]] = block.reshape(n_z, rows, VECS).astype(jnp.bfloat16)
        send(g)

    def put(o, source, value):
        out_ref[pl.ds(number(o) * n_z + source, rows, stride=27 * n_z), :] = value

    for o, k in zip(ORDER, PLACES):
        put(o, me[2], stage[me[2], k].astype(jnp.float32))
    recv[me[2], 1] = stage[me[2], 1]
    for r in NEIGHBOURS:
        copies[r].wait_send()

    for d in distances:
        receive(0, d)
        receive(len(GROUPS), d)
    few = recv[:, 1].reshape(VECS, VECS)
    from_cell = lax.broadcasted_iota(jnp.int32, (VECS, 16 * n_z), 0) // rows
    to_cell = lax.broadcasted_iota(jnp.int32, (VECS, 16 * n_z), 1) // 16
    for i, (x, y) in enumerate(CROSS):
        right = cells[:, i].reshape(n_z * 16, VECS)
        ok = inside((x, y, 0))
        for z in (-1, 0, 1):
            start = (3 * i + z + 1) * 128
            left = dot(few, choose_ref[:, start : start + 16 * n_z])
            left = jnp.where(from_cell + z == to_cell, left, 0.0).astype(jnp.bfloat16)
            block = jnp.where(ok, dot(left, right), 0.0)
            for source in range(n_z):
                put((x, y, z), source, block[source * rows : (source + 1) * rows])

    for d in reversed(distances):
        receive(1, d)
        receive(2, d)
        source = lax.rem(me[2] + n_z - d, n_z)
        for o, k in zip(ORDER, PLACES):
            put(o, source, recv[source, k].astype(jnp.float32))
    for d in distances:
        for g in range(len(GROUPS) + 1):
            rows_copy(g, d, lax.rem(me[2] + d, n_z), me[2]).wait_send()


def body(sizes, deflation, material, moduli, stencil):
    n_z = sizes[2]
    rows = VECS // n_z
    vectors = jnp.transpose(deflation, (0, 1, 3, 2, 4)).reshape(CX, PLANE, VECS)
    classes = jnp.transpose(material, (1, 2, 0)).reshape(CY * CZ, CX)
    coupling = jnp.transpose(stencil, (1, 2, 0))
    index, widen, chosen, pack, regroup, place, eye, choose = tables()
    b16 = jnp.bfloat16
    operands = (
        vectors, classes, moduli, coupling, index, widen, chosen,
        jnp.asarray(pack, b16), jnp.asarray(regroup, b16), place, jnp.asarray(eye, b16), jnp.asarray(choose, b16),
    )
    spaces = [pltpu.SMEM if k == 2 else pltpu.VMEM for k in range(len(operands))]
    out = pl.pallas_call(
        functools.partial(kernel, sizes),
        out_shape=jax.ShapeDtypeStruct((rows * 27 * n_z, VECS), jnp.float32),
        in_specs=[pl.BlockSpec(memory_space=pltpu.HBM)] * len(operands),
        out_specs=pl.BlockSpec(memory_space=pltpu.VMEM),
        scratch_shapes=[space(v.shape, v.dtype) for space, v in zip(spaces, operands)] + [
            pltpu.SemaphoreType.DMA((len(operands),)),
            pltpu.VMEM((CX + 4, PLANE, VECS), b16),
            pltpu.VMEM((5, CX, 16, VECS), b16),
            pltpu.VMEM((4, 32, VECS), b16),
            pltpu.VMEM((2, PLANE, VECS), b16),
            pltpu.VMEM((2, CX, 16, VECS), b16),
            pltpu.VMEM((2, CX, 16, VECS), b16),
            pltpu.VMEM((4, 32, VECS), b16),
            pltpu.VMEM((4, 16, VECS), b16),
            pltpu.VMEM((4, 16, VECS), b16),
            pltpu.VMEM((CX + 2, PLANE, VECS), b16),
            pltpu.VMEM((4, CX + 2, 16, VECS), b16),
            pltpu.VMEM((CX + 2, 16, VECS), b16),
            pltpu.VMEM((4, 32, VECS), b16),
            pltpu.VMEM((n_z, 16, rows, VECS), b16),
            pltpu.VMEM((n_z, 16, rows, VECS), b16),
            pltpu.VMEM((n_z, 4, 16, VECS), b16),
            pltpu.SemaphoreType.DMA((len(NEIGHBOURS),)),
            pltpu.SemaphoreType.DMA((len(NEIGHBOURS),)),
            pltpu.SemaphoreType.DMA((len(GROUPS) + 1, n_z - 1)),
            pltpu.SemaphoreType.DMA((len(GROUPS) + 1, n_z - 1)),
        ],
        compiler_params=pltpu.CompilerParams(collective_id=0, has_side_effects=True, vmem_limit_bytes=24 * 2**20),
        name="coarse",
    )(*[pltpu.with_memory_space_constraint(v, pltpu.HBM) for v in operands])
    return jnp.transpose(out.reshape(1, 1, rows, 27, n_z, VECS), (0, 1, 2, 4, 3, 5))


def solution(mesh):
    sizes = tuple(mesh.shape[name] for name in ("gx", "gy", "gz"))
    in_specs = (P("gx", "gy", "gz", None, None), P("gx", "gy", "gz"), P(), P())
    out_specs = P("gx", "gy", "gz", None, None, None)
    return jax.shard_map(
        functools.partial(body, sizes), mesh=mesh, in_specs=in_specs, out_specs=out_specs, check_vma=False
    )
```

```python
import functools

import jax
import jax.numpy as jnp
import numpy as np
from jax import lax
from jax.experimental import pallas as pl
from jax.experimental.pallas import tpu as pltpu
from jax.sharding import PartitionSpec as P

MESH = pl.DeviceIdType.MESH
HIGHEST = lax.Precision.HIGHEST
CX, CY, CZ, VECS = 8, 4, 4, 128
PLANE = CY * 3 * CZ
OFFSETS = [(i, j, k) for i in (-1, 0, 1) for j in (-1, 0, 1) for k in (-1, 0, 1)]
CROSS = [(i, j) for i in (-1, 1) for j in (-1, 1)]
NEIGHBOURS = [o for o in OFFSETS if o != (0, 0, 0) and 0 in o]
GROUPS = (
    [(0, 0, 0)],
    [o for o in NEIGHBOURS if o[1] == 0],
    [o for o in NEIGHBOURS if o[0] == 0 and o[1] != 0],
)
ORDER = [o for g in GROUPS for o in g]
SLOTS = (slice(0, 2), slice(2, 10), slice(10, 16))
PLACES = [0] + list(range(2, 16))


def number(o):
    return 9 * (o[0] + 1) + 3 * (o[1] + 1) + o[2] + 1


def side(v):
    return 1 if v > 0 else 0


def pair(v, w):
    return 2 * side(v) + side(w)


def image_rows():
    rows = [(y, z, b) for y in range(CY) for b in range(3) for z in range(CZ)]
    for y in (-1, CY):
        rows += [(y, z, b) for b in range(3) for z in range(CZ)] + [None] * 4
    for z in (-1, CZ):
        rows += [(y, z, b) for y in range(CY) for b in range(3)] + [None] * 4
    for y in (-1, CY):
        for z in (-1, CZ):
            rows += [(y, z, b) for b in range(3)] + [None]
    return rows


@functools.cache
def tables():
    rows = image_rows()
    index = np.full((128, 3 * PLANE), -1, np.int32)
    for r, row in enumerate(rows):
        if row is None:
            continue
        for p in range(3):
            for y in range(CY):
                for a in range(3):
                    for z in range(CZ):
                        oy, oz = row[0] - y, row[1] - z
                        if abs(oy) <= 1 and abs(oz) <= 1:
                            index[r, p * PLANE + y * 12 + a * 4 + z] = (3 * (oy + 1) + oz + 1) * 3 + row[2]
    widen = np.zeros((3, 27, 3 * PLANE), np.float32)
    for n in range(27):
        for y in range(CY):
            for a in range(3):
                for z in range(CZ):
                    widen[a, n, (2 - n // 9) * PLANE + y * 12 + a * 4 + z] = 1
    chosen = (np.arange(27)[None, :] % 9 == np.arange(16)[:, None]).astype(np.float32)
    pack = np.zeros((80, PLANE), np.float32)
    for r, row in enumerate(rows[48:]):
        if row is not None:
            y, z, a = row
            pack[r, (y % CY) * 12 + a * 4 + z % CZ] = 1
    regroup = np.zeros((128, 128), np.float32)
    for j in range(4):
        for x in range(CX):
            for b in range(4):
                regroup[j * 32 + x * 4 + b, x * 16 + j * 4 + b] = 1
    place = np.zeros((PLANE, 16), np.float32)
    for y in range(CY):
        for a in range(3):
            for z in range(CZ):
                place[y * 12 + a * 4 + z, y * CZ + z] = 1
    choose = np.zeros((128, 12, 8, 16), np.float32)
    for g, (_, y) in enumerate(CROSS):
        for a in range(3):
            for z in range(CZ):
                choose[g * 32 + a * 4 + z, 3 * g + 1, :, a * 4 + z] = 1
            choose[g * 32 + 16 + pair(y, -1) * 4 + a, 3 * g, :, a * 4 + CZ - 1] = 1
            choose[g * 32 + 16 + pair(y, 1) * 4 + a, 3 * g + 2, :, a * 4] = 1
    return index, widen, chosen, pack, regroup, place, np.eye(128, dtype=np.float32), choose.reshape(128, 1536)


def dot(a, b, precision=None):
    return jnp.dot(a, b, preferred_element_type=jnp.float32, precision=precision)


def contract(left, right):
    return lax.dot_general(left, right, (((0,), (0,)), ((), ())), preferred_element_type=jnp.float32)


def kernel(
    sizes,
    vec_in, mat_in, mod_in, sten_in, index_in, widen_in, chosen_in, pack_in, regroup_in, place_in, eye_in, choose_in,
    out_ref,
    vec_ref, mat_ref, mod_ref, sten_ref, index_ref, widen_ref, chosen_ref, pack_ref, regroup_ref, place_ref, eye_ref, choose_ref, load_sem,
    xp, pk, edge, hx, hy, hz, hyz, hxy, hxz, ic, iyz, icn, ie, stage, recv, cells,
    halo_send, halo_recv, row_send, row_recv,
):
    loads = [
        pltpu.make_async_copy(src, dst, load_sem.at[k])
        for k, (src, dst) in enumerate([
            (mat_in, mat_ref), (mod_in, mod_ref), (place_in, place_ref), (vec_in, vec_ref), (pack_in, pack_ref),
            (regroup_in, regroup_ref), (sten_in, sten_ref), (index_in, index_ref), (widen_in, widen_ref), (chosen_in, chosen_ref),
            (eye_in, eye_ref), (choose_in, choose_ref),
        ])
    ]
    for copy in loads:
        copy.start()
    n_z = sizes[2]
    rows = VECS // n_z
    me = (lax.axis_index("gx"), lax.axis_index("gy"), lax.axis_index("gz"))

    def at(o):
        return tuple(lax.rem(me[i] + (o[i] + sizes[i]), sizes[i]) for i in range(3))

    def inside(o):
        ok = None
        for i in range(3):
            if o[i] == 0:
                continue
            here = me[i] > 0 if o[i] < 0 else me[i] < sizes[i] - 1
            ok = here if ok is None else jnp.logical_and(ok, here)
        return ok

    barrier = pltpu.get_barrier_semaphore()
    present = jnp.int32(n_z - 1)
    for o in NEIGHBOURS:
        if o[:2] == (0, 0):
            continue
        present = present + inside(o).astype(jnp.int32)

        @pl.when(inside(o))
        def _():
            pl.semaphore_signal(barrier, inc=1, device_id=at(o), device_id_type=MESH)

    for d in range(1, n_z):
        pl.semaphore_signal(barrier, inc=1, device_id=at((0, 0, d)), device_id_type=MESH)

    for copy in loads[:6]:
        copy.wait()
    mat = mat_ref[...]
    value = jnp.zeros(mat.shape, jnp.float32)
    for c in range(16):
        value = jnp.where(mat == c, mod_ref[c], value)
    root = jnp.sqrt(value)
    wide = jnp.concatenate([jnp.broadcast_to(root[:, x : x + 1], (16, VECS)) for x in range(CX)], axis=1)
    scale = dot(place_ref[...], wide, HIGHEST)
    empty = jnp.zeros((PLANE, VECS), jnp.bfloat16)
    for i in (0, 1, CX + 2, CX + 3):
        xp[i] = empty
    for x in range(CX):
        plane = (vec_ref[x].astype(jnp.float32) * scale[:, x * VECS : (x + 1) * VECS]).astype(jnp.bfloat16)
        xp[2 + x] = plane
        packed = dot(pack_ref[...], plane)
        for k in range(5):
            pk[k, x] = packed[16 * k : 16 * k + 16].astype(jnp.bfloat16)
    dense = dot(regroup_ref[...], pk[4].reshape(CX * 16, VECS)).astype(jnp.bfloat16)
    for j in range(4):
        edge[j] = dense[32 * j : 32 * j + 32]

    pl.semaphore_wait(barrier, present)

    def halo(r):
        xi = CX - 1 if r[0] < 0 else 0
        if r[1] == 0 and r[2] == 0:
            return xp.at[2 + xi], hx.at[side(r[0])]
        if r[0] == 0 and r[2] == 0:
            return pk.at[side(r[1])], hy.at[side(r[1])]
        if r[0] == 0 and r[1] == 0:
            return pk.at[2 + side(r[2])], hz.at[side(r[2])]
        if r[0] == 0:
            return edge.at[pair(r[1], r[2])], hyz.at[pair(r[1], r[2])]
        if r[2] == 0:
            return pk.at[side(r[1]), xi], hxy.at[pair(r[0], r[1])]
        return pk.at[2 + side(r[2]), xi], hxz.at[pair(r[0], r[2])]

    copies = {}
    for r in sorted(NEIGHBOURS, key=lambda r: (r[1] == 0, -abs(r[0]) - abs(r[2]))):
        src, dst = halo(r)
        k = NEIGHBOURS.index(r)
        copies[r] = pltpu.make_async_remote_copy(
            src_ref=src, dst_ref=dst, send_sem=halo_send.at[k], recv_sem=halo_recv.at[k],
            device_id=at((-r[0], -r[1], -r[2])), device_id_type=MESH,
        )

        @pl.when(inside((-r[0], -r[1], -r[2])))
        def _():
            copies[r].start()

    for copy in loads[6:]:
        copy.wait()
    index = index_ref[...]
    matrix = jnp.zeros(index.shape, jnp.float32)
    chosen = chosen_ref[...]
    table = None
    for a in range(3):
        coupling = jnp.concatenate([chosen * sten_ref[a][b : b + 1, :] for b in range(3)], axis=0)
        term = dot(coupling, widen_ref[a], HIGHEST)
        table = term if table is None else table + term
    for b in range(3):
        for km in range(9):
            matrix = jnp.where(index == km * 3 + b, table[16 * b + km : 16 * b + km + 1, :], matrix)
    high = matrix.astype(jnp.bfloat16)
    low = (matrix - high.astype(jnp.float32)).astype(jnp.bfloat16)
    for i in range(CX + 2):
        window = xp[i : i + 3].reshape(3 * PLANE, VECS)
        image = (dot(high, window) + dot(low, window)).astype(jnp.bfloat16)
        ic[i] = image[0:48]
        for k in range(4):
            iyz[k, i] = image[48 + 16 * k : 64 + 16 * k]
        icn[i] = image[112:128]
    dense = dot(regroup_ref[...], icn[1 : CX + 1].reshape(CX * 16, VECS)).astype(jnp.bfloat16)
    for j in range(4):
        ie[j] = dense[32 * j : 32 * j + 32]

    def operands(o):
        xi = 0 if o[0] < 0 else CX + 1
        inner = slice(1, CX + 1)
        if o == (0, 0, 0):
            return ic[inner].reshape(CX * PLANE, VECS), xp[2 : CX + 2].reshape(CX * PLANE, VECS)
        if o[1] == 0 and o[2] == 0:
            return ic[xi], hx[side(o[0])]
        if o[0] == 0 and o[2] == 0:
            k = side(o[1])
            return iyz[k, inner].reshape(CX * 16, VECS), hy[k].reshape(CX * 16, VECS)
        if o[0] == 0 and o[1] == 0:
            k = side(o[2])
            return iyz[2 + k, inner].reshape(CX * 16, VECS), hz[k].reshape(CX * 16, VECS)
        if o[0] == 0:
            k = pair(o[1], o[2])
            return ie[k], hyz[k]
        return iyz[2 + side(o[2]), xi], hxz[pair(o[0], o[2])]

    def rows_copy(g, d, target, source):
        if g == len(GROUPS):
            src, dst = hxy, cells.at[source]
        else:
            slots = pl.ds(SLOTS[g].start, SLOTS[g].stop - SLOTS[g].start)
            src, dst = stage.at[target, slots], recv.at[source, slots]
        return pltpu.make_async_remote_copy(
            src_ref=src, dst_ref=dst, send_sem=row_send.at[g, d - 1], recv_sem=row_recv.at[g, d - 1],
            device_id=(me[0], me[1], target), device_id_type=MESH,
        )

    def arrive(o):
        @pl.when(inside(o))
        def _():
            copies[o].wait_recv()

    distances = sorted(range(1, n_z), key=lambda d: -min(d, n_z - d))

    def send(g):
        for d in distances:
            rows_copy(g, d, lax.rem(me[2] + d, n_z), me[2]).start()

    def receive(g, d):
        rows_copy(g, d, lax.rem(me[2] + d, n_z), lax.rem(me[2] + n_z - d, n_z)).wait_recv()

    few = [v for x, y in CROSS for v in (iyz[side(y), (CX + 1) * side(x)], icn[(CX + 1) * side(x)])]
    few = contract(jnp.concatenate(few, axis=0), eye_ref[...]).reshape(n_z, rows, VECS).astype(jnp.bfloat16)
    stage[:, 1] = few
    for g, group in enumerate(GROUPS):
        if g == 2:
            for x, y in CROSS:
                arrive((x, y, 0))
            send(len(GROUPS))
            cells[me[2]] = hxy[...]
        for o in group:
            if o in copies:
                arrive(o)
        for o in group:
            left, right = operands(o)
            block = contract(left, right)
            if o != (0, 0, 0):
                block = jnp.where(inside(o), block, 0.0)
            stage[:, PLACES[ORDER.index(o)]] = block.reshape(n_z, rows, VECS).astype(jnp.bfloat16)
        send(g)

    def put(o, source, value):
        out_ref[pl.ds(number(o) * n_z + source, rows, stride=27 * n_z), :] = value

    for o, k in zip(ORDER, PLACES):
        put(o, me[2], stage[me[2], k].astype(jnp.float32))
    recv[me[2], 1] = stage[me[2], 1]
    for r in NEIGHBOURS:

        @pl.when(inside((-r[0], -r[1], -r[2])))
        def _():
            copies[r].wait_send()

    for d in distances:
        receive(0, d)
        receive(len(GROUPS), d)
    few = recv[:, 1].reshape(VECS, VECS)
    from_cell = lax.broadcasted_iota(jnp.int32, (VECS, 16 * n_z), 0) // rows
    to_cell = lax.broadcasted_iota(jnp.int32, (VECS, 16 * n_z), 1) // 16
    for i, (x, y) in enumerate(CROSS):
        right = cells[:, i].reshape(n_z * 16, VECS)
        ok = inside((x, y, 0))
        for z in (-1, 0, 1):
            start = (3 * i + z + 1) * 128
            left = dot(few, choose_ref[:, start : start + 16 * n_z])
            left = jnp.where(from_cell + z == to_cell, left, 0.0).astype(jnp.bfloat16)
            block = jnp.where(ok, dot(left, right), 0.0)
            for source in range(n_z):
                put((x, y, z), source, block[source * rows : (source + 1) * rows])

    for d in reversed(distances):
        receive(1, d)
        receive(2, d)
        source = lax.rem(me[2] + n_z - d, n_z)
        for o, k in zip(ORDER, PLACES):
            put(o, source, recv[source, k].astype(jnp.float32))
    for d in distances:
        for g in range(len(GROUPS) + 1):
            rows_copy(g, d, lax.rem(me[2] + d, n_z), me[2]).wait_send()


def body(sizes, deflation, material, moduli, stencil):
    n_z = sizes[2]
    rows = VECS // n_z
    vectors = jnp.transpose(deflation, (0, 1, 3, 2, 4)).reshape(CX, PLANE, VECS)
    classes = jnp.transpose(material, (1, 2, 0)).reshape(CY * CZ, CX)
    coupling = jnp.transpose(stencil, (1, 2, 0))
    index, widen, chosen, pack, regroup, place, eye, choose = tables()
    b16 = jnp.bfloat16
    operands = (
        vectors, classes, moduli, coupling, index, widen, chosen,
        jnp.asarray(pack, b16), jnp.asarray(regroup, b16), place, jnp.asarray(eye, b16), jnp.asarray(choose, b16),
    )
    spaces = [pltpu.SMEM if k == 2 else pltpu.VMEM for k in range(len(operands))]
    out = pl.pallas_call(
        functools.partial(kernel, sizes),
        out_shape=jax.ShapeDtypeStruct((rows * 27 * n_z, VECS), jnp.float32),
        in_specs=[pl.BlockSpec(memory_space=pltpu.HBM)] * len(operands),
        out_specs=pl.BlockSpec(memory_space=pltpu.VMEM),
        scratch_shapes=[space(v.shape, v.dtype) for space, v in zip(spaces, operands)] + [
            pltpu.SemaphoreType.DMA((len(operands),)),
            pltpu.VMEM((CX + 4, PLANE, VECS), b16),
            pltpu.VMEM((5, CX, 16, VECS), b16),
            pltpu.VMEM((4, 32, VECS), b16),
            pltpu.VMEM((2, PLANE, VECS), b16),
            pltpu.VMEM((2, CX, 16, VECS), b16),
            pltpu.VMEM((2, CX, 16, VECS), b16),
            pltpu.VMEM((4, 32, VECS), b16),
            pltpu.VMEM((4, 16, VECS), b16),
            pltpu.VMEM((4, 16, VECS), b16),
            pltpu.VMEM((CX + 2, PLANE, VECS), b16),
            pltpu.VMEM((4, CX + 2, 16, VECS), b16),
            pltpu.VMEM((CX + 2, 16, VECS), b16),
            pltpu.VMEM((4, 32, VECS), b16),
            pltpu.VMEM((n_z, 16, rows, VECS), b16),
            pltpu.VMEM((n_z, 16, rows, VECS), b16),
            pltpu.VMEM((n_z, 4, 16, VECS), b16),
            pltpu.SemaphoreType.DMA((len(NEIGHBOURS),)),
            pltpu.SemaphoreType.DMA((len(NEIGHBOURS),)),
            pltpu.SemaphoreType.DMA((len(GROUPS) + 1, n_z - 1)),
            pltpu.SemaphoreType.DMA((len(GROUPS) + 1, n_z - 1)),
        ],
        compiler_params=pltpu.CompilerParams(collective_id=0, has_side_effects=True, vmem_limit_bytes=24 * 2**20),
        name="coarse",
    )(*[pltpu.with_memory_space_constraint(v, pltpu.HBM) for v in operands])
    return jnp.transpose(out.reshape(1, 1, rows, 27, n_z, VECS), (0, 1, 2, 4, 3, 5))


def solution(mesh):
    sizes = tuple(mesh.shape[name] for name in ("gx", "gy", "gz"))
    in_specs = (P("gx", "gy", "gz", None, None), P("gx", "gy", "gz"), P(), P())
    out_specs = P("gx", "gy", "gz", None, None, None)
    return jax.shard_map(
        functools.partial(body, sizes), mesh=mesh, in_specs=in_specs, out_specs=out_specs, check_vma=False
    )
```

```python
import functools

import jax
import jax.numpy as jnp
import numpy as np
from jax import lax
from jax.experimental import pallas as pl
from jax.experimental.pallas import tpu as pltpu
from jax.sharding import PartitionSpec as P

MESH = pl.DeviceIdType.MESH
HIGHEST = lax.Precision.HIGHEST
CX, CY, CZ, VECS = 8, 4, 4, 128
PLANE = CY * 3 * CZ
OFFSETS = [(i, j, k) for i in (-1, 0, 1) for j in (-1, 0, 1) for k in (-1, 0, 1)]
CROSS = [(i, j) for i in (-1, 1) for j in (-1, 1)]
NEIGHBOURS = [o for o in OFFSETS if o != (0, 0, 0) and 0 in o]
GROUPS = (
    [(0, 0, 0)],
    [o for o in NEIGHBOURS if o[1] == 0],
    [o for o in NEIGHBOURS if o[0] == 0 and o[1] != 0],
)
ORDER = [o for g in GROUPS for o in g]
SLOTS = (slice(0, 2), slice(2, 10), slice(10, 16))
PLACES = [0] + list(range(2, 16))


def number(o):
    return 9 * (o[0] + 1) + 3 * (o[1] + 1) + o[2] + 1


def side(v):
    return 1 if v > 0 else 0


def pair(v, w):
    return 2 * side(v) + side(w)


def image_rows():
    rows = [(y, z, b) for y in range(CY) for b in range(3) for z in range(CZ)]
    for y in (-1, CY):
        rows += [(y, z, b) for b in range(3) for z in range(CZ)] + [None] * 4
    for z in (-1, CZ):
        rows += [(y, z, b) for y in range(CY) for b in range(3)] + [None] * 4
    for y in (-1, CY):
        for z in (-1, CZ):
            rows += [(y, z, b) for b in range(3)] + [None]
    return rows


@functools.cache
def tables():
    rows = image_rows()
    index = np.full((128, 3 * PLANE), -1, np.int32)
    for r, row in enumerate(rows):
        if row is None:
            continue
        for p in range(3):
            for y in range(CY):
                for a in range(3):
                    for z in range(CZ):
                        oy, oz = row[0] - y, row[1] - z
                        if abs(oy) <= 1 and abs(oz) <= 1:
                            index[r, p * PLANE + y * 12 + a * 4 + z] = (3 * (oy + 1) + oz + 1) * 3 + row[2]
    widen = np.zeros((3, 27, 3 * PLANE), np.float32)
    for n in range(27):
        for y in range(CY):
            for a in range(3):
                for z in range(CZ):
                    widen[a, n, (2 - n // 9) * PLANE + y * 12 + a * 4 + z] = 1
    chosen = (np.arange(27)[None, :] % 9 == np.arange(16)[:, None]).astype(np.float32)
    pack = np.zeros((80, PLANE), np.float32)
    for r, row in enumerate(rows[48:]):
        if row is not None:
            y, z, a = row
            pack[r, (y % CY) * 12 + a * 4 + z % CZ] = 1
    regroup = np.zeros((128, 128), np.float32)
    for j in range(4):
        for x in range(CX):
            for b in range(4):
                regroup[j * 32 + x * 4 + b, x * 16 + j * 4 + b] = 1
    place = np.zeros((PLANE, 16), np.float32)
    for y in range(CY):
        for a in range(3):
            for z in range(CZ):
                place[y * 12 + a * 4 + z, y * CZ + z] = 1
    choose = np.zeros((128, 12, 8, 16), np.float32)
    for g, (_, y) in enumerate(CROSS):
        for a in range(3):
            for z in range(CZ):
                choose[g * 32 + a * 4 + z, 3 * g + 1, :, a * 4 + z] = 1
            choose[g * 32 + 16 + pair(y, -1) * 4 + a, 3 * g, :, a * 4 + CZ - 1] = 1
            choose[g * 32 + 16 + pair(y, 1) * 4 + a, 3 * g + 2, :, a * 4] = 1
    return index, widen, chosen, pack, regroup, place, np.eye(128, dtype=np.float32), choose.reshape(128, 1536)


def dot(a, b, precision=None):
    return jnp.dot(a, b, preferred_element_type=jnp.float32, precision=precision)


def contract(left, right):
    return lax.dot_general(left, right, (((0,), (0,)), ((), ())), preferred_element_type=jnp.float32)


def kernel(
    sizes,
    vec_in, mat_in, mod_in, sten_in, index_in, widen_in, chosen_in, pack_in, regroup_in, place_in, eye_in, choose_in,
    out_ref,
    vec_ref, mat_ref, mod_ref, sten_ref, index_ref, widen_ref, chosen_ref, pack_ref, regroup_ref, place_ref, eye_ref, choose_ref, load_sem,
    xp, pk, edge, hx, hy, hz, hyz, hxy, hxz, ic, iyz, icn, ie, stage, recv, cells,
    halo_send, halo_recv, row_send, row_recv, ready, origin_ready,
):
    loads = [
        pltpu.make_async_copy(src, dst, load_sem.at[k])
        for k, (src, dst) in enumerate([
            (mat_in, mat_ref), (mod_in, mod_ref), (place_in, place_ref), (vec_in, vec_ref), (pack_in, pack_ref),
            (regroup_in, regroup_ref), (sten_in, sten_ref), (index_in, index_ref), (widen_in, widen_ref), (chosen_in, chosen_ref),
            (eye_in, eye_ref), (choose_in, choose_ref),
        ])
    ]
    for copy in loads:
        copy.start()
    n_z = sizes[2]
    rows = VECS // n_z
    me = (lax.axis_index("gx"), lax.axis_index("gy"), lax.axis_index("gz"))

    def at(o):
        return tuple(lax.rem(me[i] + (o[i] + sizes[i]), sizes[i]) for i in range(3))

    def inside(o):
        ok = None
        for i in range(3):
            if o[i] == 0:
                continue
            here = me[i] > 0 if o[i] < 0 else me[i] < sizes[i] - 1
            ok = here if ok is None else jnp.logical_and(ok, here)
        return ok

    both, negate = jnp.logical_and, jnp.logical_not
    origin_line = both(me[0] == 0, me[1] == 0)
    origin = both(origin_line, me[2] == 0)

    def to_origin(o):
        if max(o) > 0:
            return None
        return both(both(me[0] + o[0] == 0, me[1] + o[1] == 0), me[2] + o[2] == 0)

    def except_origin(o):
        return inside(o) if max(o) > 0 else both(inside(o), negate(to_origin(o)))

    beside = [o for o in NEIGHBOURS if o[:2] != (0, 0)]
    barrier = pltpu.get_barrier_semaphore()
    expected = jnp.int32(n_z - 1) - both(origin_line, negate(origin)).astype(jnp.int32)
    for o in beside:
        awaited = both(inside(o), origin) if o[1] > 0 else except_origin(o)
        expected = expected + awaited.astype(jnp.int32)
        told = inside(o) if o[1] >= 0 else to_origin(o)
        if told is None:
            continue

        @pl.when(both(told, negate(origin)))
        def _():
            pl.semaphore_signal(barrier, inc=1, device_id=at(o), device_id_type=MESH)

    @pl.when(negate(origin))
    def _():
        for d in range(1, n_z):
            pl.semaphore_signal(barrier, inc=1, device_id=at((0, 0, d)), device_id_type=MESH)

    for copy in loads[:6]:
        copy.wait()
    mat = mat_ref[...]
    value = jnp.zeros(mat.shape, jnp.float32)
    for c in range(16):
        value = jnp.where(mat == c, mod_ref[c], value)
    root = jnp.sqrt(value)
    wide = jnp.concatenate([jnp.broadcast_to(root[:, x : x + 1], (16, VECS)) for x in range(CX)], axis=1)
    scale = dot(place_ref[...], wide, HIGHEST)
    empty = jnp.zeros((PLANE, VECS), jnp.bfloat16)
    for i in (0, 1, CX + 2, CX + 3):
        xp[i] = empty
    for x in range(CX):
        plane = (vec_ref[x].astype(jnp.float32) * scale[:, x * VECS : (x + 1) * VECS]).astype(jnp.bfloat16)
        xp[2 + x] = plane
        packed = dot(pack_ref[...], plane)
        for k in range(5):
            pk[k, x] = packed[16 * k : 16 * k + 16].astype(jnp.bfloat16)
    dense = dot(regroup_ref[...], pk[4].reshape(CX * 16, VECS)).astype(jnp.bfloat16)
    for j in range(4):
        edge[j] = dense[32 * j : 32 * j + 32]

    for copy in loads[6:]:
        copy.wait()
    index = index_ref[...]
    matrix = jnp.zeros(index.shape, jnp.float32)
    chosen = chosen_ref[...]
    table = None
    for a in range(3):
        coupling = jnp.concatenate([chosen * sten_ref[a][b : b + 1, :] for b in range(3)], axis=0)
        term = dot(coupling, widen_ref[a], HIGHEST)
        table = term if table is None else table + term
    for b in range(3):
        for km in range(9):
            matrix = jnp.where(index == km * 3 + b, table[16 * b + km : 16 * b + km + 1, :], matrix)
    high = matrix.astype(jnp.bfloat16)
    low = (matrix - high.astype(jnp.float32)).astype(jnp.bfloat16)
    pl.semaphore_wait(barrier, expected)
    for o in beside:
        if o[1] < 0:

            @pl.when(except_origin(o))
            def _():
                pl.semaphore_signal(ready, inc=1, device_id=at(o), device_id_type=MESH)

    @pl.when(origin)
    def _():
        for o in beside:
            if min(o) >= 0:
                pl.semaphore_signal(origin_ready, inc=1, device_id=at(o), device_id_type=MESH)
        for d in range(1, n_z):
            pl.semaphore_signal(origin_ready, inc=1, device_id=at((0, 0, d)), device_id_type=MESH)

    def halo(r):
        xi = CX - 1 if r[0] < 0 else 0
        if r[1] == 0 and r[2] == 0:
            return xp.at[2 + xi], hx.at[side(r[0])]
        if r[0] == 0 and r[2] == 0:
            return pk.at[side(r[1])], hy.at[side(r[1])]
        if r[0] == 0 and r[1] == 0:
            return pk.at[2 + side(r[2])], hz.at[side(r[2])]
        if r[0] == 0:
            return edge.at[pair(r[1], r[2])], hyz.at[pair(r[1], r[2])]
        if r[2] == 0:
            return pk.at[side(r[1]), xi], hxy.at[pair(r[0], r[1])]
        return pk.at[2 + side(r[2]), xi], hxz.at[pair(r[0], r[2])]

    copies = {}
    for r in sorted(NEIGHBOURS, key=lambda r: (r[1] == 0, -abs(r[0]) - abs(r[2]))):
        src, dst = halo(r)
        k = NEIGHBOURS.index(r)
        copies[r] = pltpu.make_async_remote_copy(
            src_ref=src, dst_ref=dst, send_sem=halo_send.at[k], recv_sem=halo_recv.at[k],
            device_id=at((-r[0], -r[1], -r[2])), device_id_type=MESH,
        )
        o = (-r[0], -r[1], -r[2])

        @pl.when(both(inside(o), origin) if o[1] > 0 else except_origin(o))
        def _():
            copies[r].start()

    def to_the_origin(level):
        for r in NEIGHBOURS:
            if min(r) >= 0 and r[1] == level:

                @pl.when(to_origin((-r[0], -r[1], -r[2])))
                def _():
                    pl.semaphore_wait(origin_ready, 1)
                    copies[r].start()

    def up():
        above = [o for o in beside if o[1] > 0]

        @pl.when(both(inside((0, 1, 0)), negate(origin)))
        def _():
            pl.semaphore_wait(ready, sum(inside(o).astype(jnp.int32) for o in above))

        for o in above:

            @pl.when(both(inside(o), negate(origin)))
            def _():
                copies[-o[0], -o[1], -o[2]].start()

    for i in range(CX + 2):
        window = xp[i : i + 3].reshape(3 * PLANE, VECS)
        image = (dot(high, window) + dot(low, window)).astype(jnp.bfloat16)
        ic[i] = image[0:48]
        for k in range(4):
            iyz[k, i] = image[48 + 16 * k : 64 + 16 * k]
        icn[i] = image[112:128]
    dense = dot(regroup_ref[...], icn[1 : CX + 1].reshape(CX * 16, VECS)).astype(jnp.bfloat16)
    for j in range(4):
        ie[j] = dense[32 * j : 32 * j + 32]

    def operands(o):
        xi = 0 if o[0] < 0 else CX + 1
        inner = slice(1, CX + 1)
        if o == (0, 0, 0):
            return ic[inner].reshape(CX * PLANE, VECS), xp[2 : CX + 2].reshape(CX * PLANE, VECS)
        if o[1] == 0 and o[2] == 0:
            return ic[xi], hx[side(o[0])]
        if o[0] == 0 and o[2] == 0:
            k = side(o[1])
            return iyz[k, inner].reshape(CX * 16, VECS), hy[k].reshape(CX * 16, VECS)
        if o[0] == 0 and o[1] == 0:
            k = side(o[2])
            return iyz[2 + k, inner].reshape(CX * 16, VECS), hz[k].reshape(CX * 16, VECS)
        if o[0] == 0:
            k = pair(o[1], o[2])
            return ie[k], hyz[k]
        return iyz[2 + side(o[2]), xi], hxz[pair(o[0], o[2])]

    def rows_copy(g, d, target, source):
        if g == len(GROUPS):
            src, dst = hxy, cells.at[source]
        else:
            slots = pl.ds(SLOTS[g].start, SLOTS[g].stop - SLOTS[g].start)
            src, dst = stage.at[target, slots], recv.at[source, slots]
        return pltpu.make_async_remote_copy(
            src_ref=src, dst_ref=dst, send_sem=row_send.at[g, d - 1], recv_sem=row_recv.at[g, d - 1],
            device_id=(me[0], me[1], target), device_id_type=MESH,
        )

    def arrive(o):
        @pl.when(inside(o))
        def _():
            copies[o].wait_recv()

    distances = sorted(range(1, n_z), key=lambda d: -min(d, n_z - d))

    def send(g):
        for d in distances:
            target = lax.rem(me[2] + d, n_z)

            @pl.when(negate(both(origin_line, target == 0)))
            def _():
                rows_copy(g, d, target, me[2]).start()

    def receive(g, d):
        rows_copy(g, d, lax.rem(me[2] + d, n_z), lax.rem(me[2] + n_z - d, n_z)).wait_recv()

    few = [v for x, y in CROSS for v in (iyz[side(y), (CX + 1) * side(x)], icn[(CX + 1) * side(x)])]
    few = contract(jnp.concatenate(few, axis=0), eye_ref[...]).reshape(n_z, rows, VECS).astype(jnp.bfloat16)
    stage[:, 1] = few
    for g, group in enumerate(GROUPS):
        if g == 1:
            to_the_origin(0)
        if g == 2:
            up()
            to_the_origin(1)
            for x, y in CROSS:
                arrive((x, y, 0))
            send(len(GROUPS))
            cells[me[2]] = hxy[...]
        for o in group:
            if o in copies:
                arrive(o)
        for o in group:
            left, right = operands(o)
            block = contract(left, right)
            if o != (0, 0, 0):
                block = jnp.where(inside(o), block, 0.0)
            stage[:, PLACES[ORDER.index(o)]] = block.reshape(n_z, rows, VECS).astype(jnp.bfloat16)
        send(g)

    @pl.when(both(origin_line, negate(origin)))
    def _():
        @pl.when(me[2] != 1)
        def _():
            pl.semaphore_wait(origin_ready, 1)

        for g in (0, 3, 1, 2):
            rows_copy(g, n_z - me[2], 0, me[2]).start()

    def put(o, source, value):
        out_ref[pl.ds(number(o) * n_z + source, rows, stride=27 * n_z), :] = value

    for o, k in zip(ORDER, PLACES):
        put(o, me[2], stage[me[2], k].astype(jnp.float32))
    recv[me[2], 1] = stage[me[2], 1]
    for r in NEIGHBOURS:

        @pl.when(inside((-r[0], -r[1], -r[2])))
        def _():
            copies[r].wait_send()

    for d in distances:
        receive(0, d)
        receive(len(GROUPS), d)
    few = recv[:, 1].reshape(VECS, VECS)
    from_cell = lax.broadcasted_iota(jnp.int32, (VECS, 16 * n_z), 0) // rows
    to_cell = lax.broadcasted_iota(jnp.int32, (VECS, 16 * n_z), 1) // 16
    for i, (x, y) in enumerate(CROSS):
        right = cells[:, i].reshape(n_z * 16, VECS)
        ok = inside((x, y, 0))
        for z in (-1, 0, 1):
            start = (3 * i + z + 1) * 128
            left = dot(few, choose_ref[:, start : start + 16 * n_z])
            left = jnp.where(from_cell + z == to_cell, left, 0.0).astype(jnp.bfloat16)
            block = jnp.where(ok, dot(left, right), 0.0)
            for source in range(n_z):
                put((x, y, z), source, block[source * rows : (source + 1) * rows])

    for d in reversed(distances):
        receive(1, d)
        receive(2, d)
        source = lax.rem(me[2] + n_z - d, n_z)
        for o, k in zip(ORDER, PLACES):
            put(o, source, recv[source, k].astype(jnp.float32))
    for d in distances:
        for g in range(len(GROUPS) + 1):
            rows_copy(g, d, lax.rem(me[2] + d, n_z), me[2]).wait_send()


def body(sizes, deflation, material, moduli, stencil):
    n_z = sizes[2]
    rows = VECS // n_z
    vectors = jnp.transpose(deflation, (0, 1, 3, 2, 4)).reshape(CX, PLANE, VECS)
    classes = jnp.transpose(material, (1, 2, 0)).reshape(CY * CZ, CX)
    coupling = jnp.transpose(stencil, (1, 2, 0))
    index, widen, chosen, pack, regroup, place, eye, choose = tables()
    b16 = jnp.bfloat16
    operands = (
        vectors, classes, moduli, coupling, index, widen, chosen,
        jnp.asarray(pack, b16), jnp.asarray(regroup, b16), place, jnp.asarray(eye, b16), jnp.asarray(choose, b16),
    )
    spaces = [pltpu.SMEM if k == 2 else pltpu.VMEM for k in range(len(operands))]
    out = pl.pallas_call(
        functools.partial(kernel, sizes),
        out_shape=jax.ShapeDtypeStruct((rows * 27 * n_z, VECS), jnp.float32),
        in_specs=[pl.BlockSpec(memory_space=pltpu.HBM)] * len(operands),
        out_specs=pl.BlockSpec(memory_space=pltpu.VMEM),
        scratch_shapes=[space(v.shape, v.dtype) for space, v in zip(spaces, operands)] + [
            pltpu.SemaphoreType.DMA((len(operands),)),
            pltpu.VMEM((CX + 4, PLANE, VECS), b16),
            pltpu.VMEM((5, CX, 16, VECS), b16),
            pltpu.VMEM((4, 32, VECS), b16),
            pltpu.VMEM((2, PLANE, VECS), b16),
            pltpu.VMEM((2, CX, 16, VECS), b16),
            pltpu.VMEM((2, CX, 16, VECS), b16),
            pltpu.VMEM((4, 32, VECS), b16),
            pltpu.VMEM((4, 16, VECS), b16),
            pltpu.VMEM((4, 16, VECS), b16),
            pltpu.VMEM((CX + 2, PLANE, VECS), b16),
            pltpu.VMEM((4, CX + 2, 16, VECS), b16),
            pltpu.VMEM((CX + 2, 16, VECS), b16),
            pltpu.VMEM((4, 32, VECS), b16),
            pltpu.VMEM((n_z, 16, rows, VECS), b16),
            pltpu.VMEM((n_z, 16, rows, VECS), b16),
            pltpu.VMEM((n_z, 4, 16, VECS), b16),
            pltpu.SemaphoreType.DMA((len(NEIGHBOURS),)),
            pltpu.SemaphoreType.DMA((len(NEIGHBOURS),)),
            pltpu.SemaphoreType.DMA((len(GROUPS) + 1, n_z - 1)),
            pltpu.SemaphoreType.DMA((len(GROUPS) + 1, n_z - 1)),
            pltpu.SemaphoreType.REGULAR,
            pltpu.SemaphoreType.REGULAR,
        ],
        compiler_params=pltpu.CompilerParams(collective_id=0, has_side_effects=True, vmem_limit_bytes=24 * 2**20),
        name="coarse",
    )(*[pltpu.with_memory_space_constraint(v, pltpu.HBM) for v in operands])
    return jnp.transpose(out.reshape(1, 1, rows, 27, n_z, VECS), (0, 1, 2, 4, 3, 5))


def solution(mesh):
    sizes = tuple(mesh.shape[name] for name in ("gx", "gy", "gz"))
    in_specs = (P("gx", "gy", "gz", None, None), P("gx", "gy", "gz"), P(), P())
    out_specs = P("gx", "gy", "gz", None, None, None)
    return jax.shard_map(
        functools.partial(body, sizes), mesh=mesh, in_specs=in_specs, out_specs=out_specs, check_vma=False
    )
```

```python
import functools

import jax
import jax.numpy as jnp
import numpy as np
from jax import lax
from jax.experimental import pallas as pl
from jax.experimental.pallas import tpu as pltpu
from jax.sharding import PartitionSpec as P

MESH = pl.DeviceIdType.MESH
HIGHEST = lax.Precision.HIGHEST
CX, CY, CZ, VECS = 8, 4, 4, 128
PLANE = CY * 3 * CZ
OFFSETS = [(i, j, k) for i in (-1, 0, 1) for j in (-1, 0, 1) for k in (-1, 0, 1)]
CROSS = [(i, j) for i in (-1, 1) for j in (-1, 1)]
NEIGHBOURS = [o for o in OFFSETS if o != (0, 0, 0) and 0 in o]
GROUPS = (
    [(0, 0, 0)],
    [o for o in NEIGHBOURS if o[1] == 0],
    [o for o in NEIGHBOURS if o[0] == 0 and o[1] != 0],
)
ORDER = [o for g in GROUPS for o in g]
SLOTS = (slice(0, 2), slice(2, 10), slice(10, 16))
PLACES = [0] + list(range(2, 16))


def number(o):
    return 9 * (o[0] + 1) + 3 * (o[1] + 1) + o[2] + 1


def side(v):
    return 1 if v > 0 else 0


def pair(v, w):
    return 2 * side(v) + side(w)


def image_rows():
    rows = [(y, z, b) for y in range(CY) for b in range(3) for z in range(CZ)]
    for y in (-1, CY):
        rows += [(y, z, b) for b in range(3) for z in range(CZ)] + [None] * 4
    for z in (-1, CZ):
        rows += [(y, z, b) for y in range(CY) for b in range(3)] + [None] * 4
    for y in (-1, CY):
        for z in (-1, CZ):
            rows += [(y, z, b) for b in range(3)] + [None]
    return rows


@functools.cache
def tables():
    rows = image_rows()
    index = np.full((128, 3 * PLANE), -1, np.int32)
    for r, row in enumerate(rows):
        if row is None:
            continue
        for p in range(3):
            for y in range(CY):
                for a in range(3):
                    for z in range(CZ):
                        oy, oz = row[0] - y, row[1] - z
                        if abs(oy) <= 1 and abs(oz) <= 1:
                            index[r, p * PLANE + y * 12 + a * 4 + z] = (3 * (oy + 1) + oz + 1) * 3 + row[2]
    widen = np.zeros((3, 27, 3 * PLANE), np.float32)
    for n in range(27):
        for y in range(CY):
            for a in range(3):
                for z in range(CZ):
                    widen[a, n, (2 - n // 9) * PLANE + y * 12 + a * 4 + z] = 1
    chosen = (np.arange(27)[None, :] % 9 == np.arange(16)[:, None]).astype(np.float32)
    pack = np.zeros((80, PLANE), np.float32)
    for r, row in enumerate(rows[48:]):
        if row is not None:
            y, z, a = row
            pack[r, (y % CY) * 12 + a * 4 + z % CZ] = 1
    regroup = np.zeros((128, 128), np.float32)
    for j in range(4):
        for x in range(CX):
            for b in range(4):
                regroup[j * 32 + x * 4 + b, x * 16 + j * 4 + b] = 1
    place = np.zeros((PLANE, 16), np.float32)
    for y in range(CY):
        for a in range(3):
            for z in range(CZ):
                place[y * 12 + a * 4 + z, y * CZ + z] = 1
    choose = np.zeros((128, 12, 8, 16), np.float32)
    for g, (_, y) in enumerate(CROSS):
        for a in range(3):
            for z in range(CZ):
                choose[g * 32 + a * 4 + z, 3 * g + 1, :, a * 4 + z] = 1
            choose[g * 32 + 16 + pair(y, -1) * 4 + a, 3 * g, :, a * 4 + CZ - 1] = 1
            choose[g * 32 + 16 + pair(y, 1) * 4 + a, 3 * g + 2, :, a * 4] = 1
    return index, widen, chosen, pack, regroup, place, np.eye(128, dtype=np.float32), choose.reshape(128, 1536)


CROSSINGS = (3, 7)


def crossing(y):
    return functools.reduce(jnp.logical_or, [y == k for k in CROSSINGS])


def dot(a, b, precision=None):
    return jnp.dot(a, b, preferred_element_type=jnp.float32, precision=precision)


def contract(left, right):
    return lax.dot_general(left, right, (((0,), (0,)), ((), ())), preferred_element_type=jnp.float32)


def kernel(
    sizes,
    vec_in, mat_in, mod_in, sten_in, index_in, widen_in, chosen_in, pack_in, regroup_in, place_in, eye_in, choose_in,
    out_ref,
    vec_ref, mat_ref, mod_ref, sten_ref, index_ref, widen_ref, chosen_ref, pack_ref, regroup_ref, place_ref, eye_ref, choose_ref, load_sem,
    xp, pk, edge, hx, hy, hz, hyz, hxy, hxz, ic, iyz, icn, ie, stage, recv, cells,
    halo_send, halo_recv, row_send, row_recv, ready, origin_ready,
):
    loads = [
        pltpu.make_async_copy(src, dst, load_sem.at[k])
        for k, (src, dst) in enumerate([
            (mat_in, mat_ref), (mod_in, mod_ref), (place_in, place_ref), (vec_in, vec_ref), (pack_in, pack_ref),
            (regroup_in, regroup_ref), (sten_in, sten_ref), (index_in, index_ref), (widen_in, widen_ref), (chosen_in, chosen_ref),
            (eye_in, eye_ref), (choose_in, choose_ref),
        ])
    ]
    for copy in loads:
        copy.start()
    n_z = sizes[2]
    rows = VECS // n_z
    me = (lax.axis_index("gx"), lax.axis_index("gy"), lax.axis_index("gz"))

    def at(o):
        return tuple(lax.rem(me[i] + (o[i] + sizes[i]), sizes[i]) for i in range(3))

    def inside(o):
        ok = None
        for i in range(3):
            if o[i] == 0:
                continue
            here = me[i] > 0 if o[i] < 0 else me[i] < sizes[i] - 1
            ok = here if ok is None else jnp.logical_and(ok, here)
        return ok

    both, negate = jnp.logical_and, jnp.logical_not
    origin_line = both(me[0] == 0, me[1] == 0)
    origin = both(origin_line, me[2] == 0)

    def to_origin(o):
        if max(o) > 0:
            return None
        return both(both(me[0] + o[0] == 0, me[1] + o[1] == 0), me[2] + o[2] == 0)

    def except_origin(o):
        return inside(o) if max(o) > 0 else both(inside(o), negate(to_origin(o)))

    below_crossing, above_crossing = crossing(me[1]), crossing(me[1] - 1)
    beside = [o for o in NEIGHBOURS if o[:2] != (0, 0)]
    barrier = pltpu.get_barrier_semaphore()
    expected = jnp.int32(n_z - 1) - both(origin_line, negate(origin)).astype(jnp.int32)
    for o in beside:
        awaited = both(inside(o), negate(below_crossing)) if o[1] > 0 else except_origin(o)
        expected = expected + awaited.astype(jnp.int32)
        told = inside(o) if o[1] >= 0 else both(inside(o), negate(above_crossing))

        @pl.when(both(told, negate(origin)))
        def _():
            pl.semaphore_signal(barrier, inc=1, device_id=at(o), device_id_type=MESH)

    @pl.when(negate(origin))
    def _():
        for d in range(1, n_z):
            pl.semaphore_signal(barrier, inc=1, device_id=at((0, 0, d)), device_id_type=MESH)

    @pl.when(origin)
    def _():
        pl.semaphore_wait(barrier, expected)
        for o in beside:
            if min(o) >= 0:
                pl.semaphore_signal(origin_ready, inc=1, device_id=at(o), device_id_type=MESH)
        for d in range(1, n_z):
            pl.semaphore_signal(origin_ready, inc=1, device_id=at((0, 0, d)), device_id_type=MESH)

    for copy in loads[:6]:
        copy.wait()
    mat = mat_ref[...]
    value = jnp.zeros(mat.shape, jnp.float32)
    for c in range(16):
        value = jnp.where(mat == c, mod_ref[c], value)
    root = jnp.sqrt(value)
    wide = jnp.concatenate([jnp.broadcast_to(root[:, x : x + 1], (16, VECS)) for x in range(CX)], axis=1)
    scale = dot(place_ref[...], wide, HIGHEST)
    empty = jnp.zeros((PLANE, VECS), jnp.bfloat16)
    for i in (0, 1, CX + 2, CX + 3):
        xp[i] = empty
    for x in range(CX):
        plane = (vec_ref[x].astype(jnp.float32) * scale[:, x * VECS : (x + 1) * VECS]).astype(jnp.bfloat16)
        xp[2 + x] = plane
        packed = dot(pack_ref[...], plane)
        for k in range(5):
            pk[k, x] = packed[16 * k : 16 * k + 16].astype(jnp.bfloat16)
    dense = dot(regroup_ref[...], pk[4].reshape(CX * 16, VECS)).astype(jnp.bfloat16)
    for j in range(4):
        edge[j] = dense[32 * j : 32 * j + 32]

    def halo(r):
        xi = CX - 1 if r[0] < 0 else 0
        if r[1] == 0 and r[2] == 0:
            return xp.at[2 + xi], hx.at[side(r[0])]
        if r[0] == 0 and r[2] == 0:
            return pk.at[side(r[1])], hy.at[side(r[1])]
        if r[0] == 0 and r[1] == 0:
            return pk.at[2 + side(r[2])], hz.at[side(r[2])]
        if r[0] == 0:
            return edge.at[pair(r[1], r[2])], hyz.at[pair(r[1], r[2])]
        if r[2] == 0:
            return pk.at[side(r[1]), xi], hxy.at[pair(r[0], r[1])]
        return pk.at[2 + side(r[2]), xi], hxz.at[pair(r[0], r[2])]

    copies = {}
    for r in sorted(NEIGHBOURS, key=lambda r: (r[1] == 0, -abs(r[0]) - abs(r[2]))):
        src, dst = halo(r)
        k = NEIGHBOURS.index(r)
        copies[r] = pltpu.make_async_remote_copy(
            src_ref=src, dst_ref=dst, send_sem=halo_send.at[k], recv_sem=halo_recv.at[k],
            device_id=at((-r[0], -r[1], -r[2])), device_id_type=MESH,
        )

    @pl.when(origin)
    def _():
        for r in NEIGHBOURS:
            if max(r) <= 0:
                copies[r].start()

    for copy in loads[6:]:
        copy.wait()
    index = index_ref[...]
    matrix = jnp.zeros(index.shape, jnp.float32)
    chosen = chosen_ref[...]
    table = None
    for a in range(3):
        coupling = jnp.concatenate([chosen * sten_ref[a][b : b + 1, :] for b in range(3)], axis=0)
        term = dot(coupling, widen_ref[a], HIGHEST)
        table = term if table is None else table + term
    for b in range(3):
        for km in range(9):
            matrix = jnp.where(index == km * 3 + b, table[16 * b + km : 16 * b + km + 1, :], matrix)
    high = matrix.astype(jnp.bfloat16)
    low = (matrix - high.astype(jnp.float32)).astype(jnp.bfloat16)
    @pl.when(negate(origin))
    def _():
        pl.semaphore_wait(barrier, expected)

    for o in beside:
        if o[1] < 0:

            @pl.when(both(inside(o), above_crossing))
            def _():
                pl.semaphore_signal(ready, inc=1, device_id=at(o), device_id_type=MESH)

    for r in NEIGHBOURS:
        o = (-r[0], -r[1], -r[2])
        at_once = both(inside(o), negate(below_crossing)) if o[1] > 0 else except_origin(o)

        @pl.when(both(at_once, negate(origin)))
        def _():
            copies[r].start()

    def to_the_origin(level):
        for r in NEIGHBOURS:
            if min(r) >= 0 and r[1] == level:

                @pl.when(to_origin((-r[0], -r[1], -r[2])))
                def _():
                    pl.semaphore_wait(origin_ready, 1)
                    copies[r].start()

    def up():
        above = [o for o in beside if o[1] > 0]

        @pl.when(below_crossing)
        def _():
            pl.semaphore_wait(ready, sum(inside(o).astype(jnp.int32) for o in above))

        for o in above:

            @pl.when(both(inside(o), below_crossing))
            def _():
                copies[-o[0], -o[1], -o[2]].start()

    for i in range(CX + 2):
        window = xp[i : i + 3].reshape(3 * PLANE, VECS)
        image = (dot(high, window) + dot(low, window)).astype(jnp.bfloat16)
        ic[i] = image[0:48]
        for k in range(4):
            iyz[k, i] = image[48 + 16 * k : 64 + 16 * k]
        icn[i] = image[112:128]
    dense = dot(regroup_ref[...], icn[1 : CX + 1].reshape(CX * 16, VECS)).astype(jnp.bfloat16)
    for j in range(4):
        ie[j] = dense[32 * j : 32 * j + 32]

    def operands(o):
        xi = 0 if o[0] < 0 else CX + 1
        inner = slice(1, CX + 1)
        if o == (0, 0, 0):
            return ic[inner].reshape(CX * PLANE, VECS), xp[2 : CX + 2].reshape(CX * PLANE, VECS)
        if o[1] == 0 and o[2] == 0:
            return ic[xi], hx[side(o[0])]
        if o[0] == 0 and o[2] == 0:
            k = side(o[1])
            return iyz[k, inner].reshape(CX * 16, VECS), hy[k].reshape(CX * 16, VECS)
        if o[0] == 0 and o[1] == 0:
            k = side(o[2])
            return iyz[2 + k, inner].reshape(CX * 16, VECS), hz[k].reshape(CX * 16, VECS)
        if o[0] == 0:
            k = pair(o[1], o[2])
            return ie[k], hyz[k]
        return iyz[2 + side(o[2]), xi], hxz[pair(o[0], o[2])]

    def rows_copy(g, d, target, source):
        if g == len(GROUPS):
            src, dst = hxy, cells.at[source]
        else:
            slots = pl.ds(SLOTS[g].start, SLOTS[g].stop - SLOTS[g].start)
            src, dst = stage.at[target, slots], recv.at[source, slots]
        return pltpu.make_async_remote_copy(
            src_ref=src, dst_ref=dst, send_sem=row_send.at[g, d - 1], recv_sem=row_recv.at[g, d - 1],
            device_id=(me[0], me[1], target), device_id_type=MESH,
        )

    def arrive(o):
        @pl.when(inside(o))
        def _():
            copies[o].wait_recv()

    distances = sorted(range(1, n_z), key=lambda d: -min(d, n_z - d))

    def send(g):
        for d in distances:
            target = lax.rem(me[2] + d, n_z)

            @pl.when(negate(both(origin_line, target == 0)))
            def _():
                rows_copy(g, d, target, me[2]).start()

    def receive(g, d):
        rows_copy(g, d, lax.rem(me[2] + d, n_z), lax.rem(me[2] + n_z - d, n_z)).wait_recv()

    few = [v for x, y in CROSS for v in (iyz[side(y), (CX + 1) * side(x)], icn[(CX + 1) * side(x)])]
    few = contract(jnp.concatenate(few, axis=0), eye_ref[...]).reshape(n_z, rows, VECS).astype(jnp.bfloat16)
    stage[:, 1] = few
    for g, group in enumerate(GROUPS):
        if g == 1:
            to_the_origin(0)
        if g == 2:
            up()
            to_the_origin(1)
            for x, y in CROSS:
                arrive((x, y, 0))
            send(len(GROUPS))
            cells[me[2]] = hxy[...]
        for o in group:
            if o in copies:
                arrive(o)
        for o in group:
            left, right = operands(o)
            block = contract(left, right)
            if o != (0, 0, 0):
                block = jnp.where(inside(o), block, 0.0)
            stage[:, PLACES[ORDER.index(o)]] = block.reshape(n_z, rows, VECS).astype(jnp.bfloat16)
        send(g)

    @pl.when(both(origin_line, negate(origin)))
    def _():
        @pl.when(me[2] != 1)
        def _():
            pl.semaphore_wait(origin_ready, 1)

        for g in (0, 3, 1, 2):
            rows_copy(g, n_z - me[2], 0, me[2]).start()

    def put(o, source, value):
        out_ref[pl.ds(number(o) * n_z + source, rows, stride=27 * n_z), :] = value

    for o, k in zip(ORDER, PLACES):
        put(o, me[2], stage[me[2], k].astype(jnp.float32))
    recv[me[2], 1] = stage[me[2], 1]
    for r in NEIGHBOURS:

        @pl.when(inside((-r[0], -r[1], -r[2])))
        def _():
            copies[r].wait_send()

    for d in distances:
        receive(0, d)
        receive(len(GROUPS), d)
    few = recv[:, 1].reshape(VECS, VECS)
    from_cell = lax.broadcasted_iota(jnp.int32, (VECS, 16 * n_z), 0) // rows
    to_cell = lax.broadcasted_iota(jnp.int32, (VECS, 16 * n_z), 1) // 16
    for i, (x, y) in enumerate(CROSS):
        right = cells[:, i].reshape(n_z * 16, VECS)
        ok = inside((x, y, 0))
        for z in (-1, 0, 1):
            start = (3 * i + z + 1) * 128
            left = dot(few, choose_ref[:, start : start + 16 * n_z])
            left = jnp.where(from_cell + z == to_cell, left, 0.0).astype(jnp.bfloat16)
            block = jnp.where(ok, dot(left, right), 0.0)
            for source in range(n_z):
                put((x, y, z), source, block[source * rows : (source + 1) * rows])

    for d in reversed(distances):
        receive(1, d)
        receive(2, d)
        source = lax.rem(me[2] + n_z - d, n_z)
        for o, k in zip(ORDER, PLACES):
            put(o, source, recv[source, k].astype(jnp.float32))
    for d in distances:
        for g in range(len(GROUPS) + 1):
            rows_copy(g, d, lax.rem(me[2] + d, n_z), me[2]).wait_send()


def body(sizes, deflation, material, moduli, stencil):
    n_z = sizes[2]
    rows = VECS // n_z
    vectors = jnp.transpose(deflation, (0, 1, 3, 2, 4)).reshape(CX, PLANE, VECS)
    classes = jnp.transpose(material, (1, 2, 0)).reshape(CY * CZ, CX)
    coupling = jnp.transpose(stencil, (1, 2, 0))
    index, widen, chosen, pack, regroup, place, eye, choose = tables()
    b16 = jnp.bfloat16
    operands = (
        vectors, classes, moduli, coupling, index, widen, chosen,
        jnp.asarray(pack, b16), jnp.asarray(regroup, b16), place, jnp.asarray(eye, b16), jnp.asarray(choose, b16),
    )
    spaces = [pltpu.SMEM if k == 2 else pltpu.VMEM for k in range(len(operands))]
    out = pl.pallas_call(
        functools.partial(kernel, sizes),
        out_shape=jax.ShapeDtypeStruct((rows * 27 * n_z, VECS), jnp.float32),
        in_specs=[pl.BlockSpec(memory_space=pltpu.HBM)] * len(operands),
        out_specs=pl.BlockSpec(memory_space=pltpu.VMEM),
        scratch_shapes=[space(v.shape, v.dtype) for space, v in zip(spaces, operands)] + [
            pltpu.SemaphoreType.DMA((len(operands),)),
            pltpu.VMEM((CX + 4, PLANE, VECS), b16),
            pltpu.VMEM((5, CX, 16, VECS), b16),
            pltpu.VMEM((4, 32, VECS), b16),
            pltpu.VMEM((2, PLANE, VECS), b16),
            pltpu.VMEM((2, CX, 16, VECS), b16),
            pltpu.VMEM((2, CX, 16, VECS), b16),
            pltpu.VMEM((4, 32, VECS), b16),
            pltpu.VMEM((4, 16, VECS), b16),
            pltpu.VMEM((4, 16, VECS), b16),
            pltpu.VMEM((CX + 2, PLANE, VECS), b16),
            pltpu.VMEM((4, CX + 2, 16, VECS), b16),
            pltpu.VMEM((CX + 2, 16, VECS), b16),
            pltpu.VMEM((4, 32, VECS), b16),
            pltpu.VMEM((n_z, 16, rows, VECS), b16),
            pltpu.VMEM((n_z, 16, rows, VECS), b16),
            pltpu.VMEM((n_z, 4, 16, VECS), b16),
            pltpu.SemaphoreType.DMA((len(NEIGHBOURS),)),
            pltpu.SemaphoreType.DMA((len(NEIGHBOURS),)),
            pltpu.SemaphoreType.DMA((len(GROUPS) + 1, n_z - 1)),
            pltpu.SemaphoreType.DMA((len(GROUPS) + 1, n_z - 1)),
            pltpu.SemaphoreType.REGULAR,
            pltpu.SemaphoreType.REGULAR,
        ],
        compiler_params=pltpu.CompilerParams(collective_id=0, has_side_effects=True, vmem_limit_bytes=24 * 2**20),
        name="coarse",
    )(*[pltpu.with_memory_space_constraint(v, pltpu.HBM) for v in operands])
    return jnp.transpose(out.reshape(1, 1, rows, 27, n_z, VECS), (0, 1, 2, 4, 3, 5))


def solution(mesh):
    sizes = tuple(mesh.shape[name] for name in ("gx", "gy", "gz"))
    in_specs = (P("gx", "gy", "gz", None, None), P("gx", "gy", "gz"), P(), P())
    out_specs = P("gx", "gy", "gz", None, None, None)
    return jax.shard_map(
        functools.partial(body, sizes), mesh=mesh, in_specs=in_specs, out_specs=out_specs, check_vma=False
    )
```

```python
import functools

import jax
import jax.numpy as jnp
import numpy as np
from jax import lax
from jax.experimental import pallas as pl
from jax.experimental.pallas import tpu as pltpu
from jax.sharding import PartitionSpec as P

MESH = pl.DeviceIdType.MESH
HIGHEST = lax.Precision.HIGHEST
CX, CY, CZ, VECS = 8, 4, 4, 128
PLANE = CY * 3 * CZ
OFFSETS = [(i, j, k) for i in (-1, 0, 1) for j in (-1, 0, 1) for k in (-1, 0, 1)]
CROSS = [(i, j) for i in (-1, 1) for j in (-1, 1)]
NEIGHBOURS = [o for o in OFFSETS if o != (0, 0, 0) and 0 in o]
GROUPS = (
    [(0, 0, 0)],
    [o for o in NEIGHBOURS if o[1] == 0],
    [o for o in NEIGHBOURS if o[0] == 0 and o[1] != 0],
)
ORDER = [o for g in GROUPS for o in g]
SLOTS = (slice(0, 2), slice(2, 10), slice(10, 16))
PLACES = [0] + list(range(2, 16))


def number(o):
    return 9 * (o[0] + 1) + 3 * (o[1] + 1) + o[2] + 1


def side(v):
    return 1 if v > 0 else 0


def pair(v, w):
    return 2 * side(v) + side(w)


def image_rows():
    rows = [(y, z, b) for y in range(CY) for b in range(3) for z in range(CZ)]
    for y in (-1, CY):
        rows += [(y, z, b) for b in range(3) for z in range(CZ)] + [None] * 4
    for z in (-1, CZ):
        rows += [(y, z, b) for y in range(CY) for b in range(3)] + [None] * 4
    for y in (-1, CY):
        for z in (-1, CZ):
            rows += [(y, z, b) for b in range(3)] + [None]
    return rows


@functools.cache
def tables():
    rows = image_rows()
    index = np.full((128, 3 * PLANE), -1, np.int32)
    for r, row in enumerate(rows):
        if row is None:
            continue
        for p in range(3):
            for y in range(CY):
                for a in range(3):
                    for z in range(CZ):
                        oy, oz = row[0] - y, row[1] - z
                        if abs(oy) <= 1 and abs(oz) <= 1:
                            index[r, p * PLANE + y * 12 + a * 4 + z] = (3 * (oy + 1) + oz + 1) * 3 + row[2]
    widen = np.zeros((3, 27, 3 * PLANE), np.float32)
    for n in range(27):
        for y in range(CY):
            for a in range(3):
                for z in range(CZ):
                    widen[a, n, (2 - n // 9) * PLANE + y * 12 + a * 4 + z] = 1
    chosen = (np.arange(27)[None, :] % 9 == np.arange(16)[:, None]).astype(np.float32)
    pack = np.zeros((80, PLANE), np.float32)
    for r, row in enumerate(rows[48:]):
        if row is not None:
            y, z, a = row
            pack[r, (y % CY) * 12 + a * 4 + z % CZ] = 1
    regroup = np.zeros((2, 96, 128), np.float32)
    for x in range(CX):
        for j in range(4):
            for b in range(3):
                regroup[0, j * 24 + x * 3 + b, x * 16 + j * 4 + b] = 1
        for j in range(12):
            regroup[1, x * 12 + j, x * 16 + j] = 1
    place = np.zeros((PLANE, 16), np.float32)
    for y in range(CY):
        for a in range(3):
            for z in range(CZ):
                place[y * 12 + a * 4 + z, y * CZ + z] = 1
    choose = np.zeros((128, 12, 8, 16), np.float32)
    for g, (_, y) in enumerate(CROSS):
        for a in range(3):
            for z in range(CZ):
                choose[g * 32 + a * 4 + z, 3 * g + 1, :, a * 4 + z] = 1
            choose[g * 32 + 16 + pair(y, -1) * 4 + a, 3 * g, :, a * 4 + CZ - 1] = 1
            choose[g * 32 + 16 + pair(y, 1) * 4 + a, 3 * g + 2, :, a * 4] = 1
    return index, widen, chosen, pack, regroup, place, np.eye(128, dtype=np.float32), choose.reshape(128, 1536)


CROSSINGS = (3, 7)


def crossing(y):
    return functools.reduce(jnp.logical_or, [y == k for k in CROSSINGS])


def dot(a, b, precision=None):
    return jnp.dot(a, b, preferred_element_type=jnp.float32, precision=precision)


def contract(left, right):
    return lax.dot_general(left, right, (((0,), (0,)), ((), ())), preferred_element_type=jnp.float32)


def kernel(
    sizes,
    vec_in, mat_in, mod_in, sten_in, index_in, widen_in, chosen_in, pack_in, regroup_in, place_in, eye_in, choose_in,
    out_ref,
    vec_ref, mat_ref, mod_ref, sten_ref, index_ref, widen_ref, chosen_ref, pack_ref, regroup_ref, place_ref, eye_ref, choose_ref, load_sem,
    xp, pk, edge, face, iface, hx, hy, hz, hyz, hxy, hxz, ic, iyz, icn, ie, stage, recv, cells,
    halo_send, halo_recv, row_send, row_recv, ready, origin_ready,
):
    loads = [
        pltpu.make_async_copy(src, dst, load_sem.at[k])
        for k, (src, dst) in enumerate([
            (mat_in, mat_ref), (mod_in, mod_ref), (place_in, place_ref), (vec_in, vec_ref), (pack_in, pack_ref),
            (regroup_in, regroup_ref), (sten_in, sten_ref), (index_in, index_ref), (widen_in, widen_ref), (chosen_in, chosen_ref),
            (eye_in, eye_ref), (choose_in, choose_ref),
        ])
    ]
    for copy in loads:
        copy.start()
    n_z = sizes[2]
    rows = VECS // n_z
    me = (lax.axis_index("gx"), lax.axis_index("gy"), lax.axis_index("gz"))

    def at(o):
        return tuple(lax.rem(me[i] + (o[i] + sizes[i]), sizes[i]) for i in range(3))

    def inside(o):
        ok = None
        for i in range(3):
            if o[i] == 0:
                continue
            here = me[i] > 0 if o[i] < 0 else me[i] < sizes[i] - 1
            ok = here if ok is None else jnp.logical_and(ok, here)
        return ok

    both, negate = jnp.logical_and, jnp.logical_not
    origin_line = both(me[0] == 0, me[1] == 0)
    origin = both(origin_line, me[2] == 0)

    def to_origin(o):
        if max(o) > 0:
            return None
        return both(both(me[0] + o[0] == 0, me[1] + o[1] == 0), me[2] + o[2] == 0)

    def except_origin(o):
        return inside(o) if max(o) > 0 else both(inside(o), negate(to_origin(o)))

    below_crossing, above_crossing = crossing(me[1]), crossing(me[1] - 1)
    beside = [o for o in NEIGHBOURS if o[:2] != (0, 0)]
    barrier = pltpu.get_barrier_semaphore()
    expected = jnp.int32(n_z - 1) - both(origin_line, negate(origin)).astype(jnp.int32)
    for o in beside:
        awaited = both(inside(o), negate(below_crossing)) if o[1] > 0 else except_origin(o)
        expected = expected + awaited.astype(jnp.int32)
        told = inside(o) if o[1] >= 0 else both(inside(o), negate(above_crossing))

        @pl.when(both(told, negate(origin)))
        def _():
            pl.semaphore_signal(barrier, inc=1, device_id=at(o), device_id_type=MESH)

    @pl.when(negate(origin))
    def _():
        for d in range(1, n_z):
            pl.semaphore_signal(barrier, inc=1, device_id=at((0, 0, d)), device_id_type=MESH)

    @pl.when(origin)
    def _():
        pl.semaphore_wait(barrier, expected)
        for o in beside:
            if min(o) >= 0:
                pl.semaphore_signal(origin_ready, inc=1, device_id=at(o), device_id_type=MESH)
        for d in range(1, n_z):
            pl.semaphore_signal(origin_ready, inc=1, device_id=at((0, 0, d)), device_id_type=MESH)

    for copy in loads[:6]:
        copy.wait()
    mat = mat_ref[...]
    value = jnp.zeros(mat.shape, jnp.float32)
    for c in range(16):
        value = jnp.where(mat == c, mod_ref[c], value)
    root = jnp.sqrt(value)
    wide = jnp.concatenate([jnp.broadcast_to(root[:, x : x + 1], (16, VECS)) for x in range(CX)], axis=1)
    scale = dot(place_ref[...], wide, HIGHEST)
    empty = jnp.zeros((PLANE, VECS), jnp.bfloat16)
    for i in (0, 1, CX + 2, CX + 3):
        xp[i] = empty
    for x in range(CX):
        plane = (vec_ref[x].astype(jnp.float32) * scale[:, x * VECS : (x + 1) * VECS]).astype(jnp.bfloat16)
        xp[2 + x] = plane
        packed = dot(pack_ref[...], plane)
        for k in range(5):
            pk[k, x] = packed[16 * k : 16 * k + 16].astype(jnp.bfloat16)
    dense = dot(regroup_ref[0], pk[4].reshape(CX * 16, VECS))
    for j in range(4):
        edge[j] = dense[24 * j : 24 * j + 24].astype(jnp.bfloat16)
        face[j] = dot(regroup_ref[1], pk[j].reshape(CX * 16, VECS)).astype(jnp.bfloat16)

    def halo(r):
        xi = CX - 1 if r[0] < 0 else 0
        if r[1] == 0 and r[2] == 0:
            return xp.at[2 + xi], hx.at[side(r[0])]
        if r[0] == 0 and r[2] == 0:
            return face.at[side(r[1])], hy.at[side(r[1])]
        if r[0] == 0 and r[1] == 0:
            return face.at[2 + side(r[2])], hz.at[side(r[2])]
        if r[0] == 0:
            return edge.at[pair(r[1], r[2])], hyz.at[pair(r[1], r[2])]
        if r[2] == 0:
            return pk.at[side(r[1]), xi], hxy.at[pair(r[0], r[1])]
        return pk.at[2 + side(r[2]), xi], hxz.at[pair(r[0], r[2])]

    copies = {}
    for r in sorted(NEIGHBOURS, key=lambda r: (r[1] == 0, -abs(r[0]) - abs(r[2]))):
        src, dst = halo(r)
        k = NEIGHBOURS.index(r)
        copies[r] = pltpu.make_async_remote_copy(
            src_ref=src, dst_ref=dst, send_sem=halo_send.at[k], recv_sem=halo_recv.at[k],
            device_id=at((-r[0], -r[1], -r[2])), device_id_type=MESH,
        )

    @pl.when(origin)
    def _():
        for r in NEIGHBOURS:
            if max(r) <= 0:
                copies[r].start()

    @pl.when(negate(origin))
    def _():
        pl.semaphore_wait(barrier, expected)

    for o in beside:
        if o[1] < 0:

            @pl.when(both(inside(o), above_crossing))
            def _():
                pl.semaphore_signal(ready, inc=1, device_id=at(o), device_id_type=MESH)

    for r in NEIGHBOURS:
        o = (-r[0], -r[1], -r[2])
        at_once = both(inside(o), negate(below_crossing)) if o[1] > 0 else except_origin(o)

        @pl.when(both(at_once, negate(origin)))
        def _():
            copies[r].start()

    def to_the_origin(level):
        for r in NEIGHBOURS:
            if min(r) >= 0 and r[1] == level:

                @pl.when(to_origin((-r[0], -r[1], -r[2])))
                def _():
                    pl.semaphore_wait(origin_ready, 1)
                    copies[r].start()

    def up():
        above = [o for o in beside if o[1] > 0]

        @pl.when(below_crossing)
        def _():
            pl.semaphore_wait(ready, sum(inside(o).astype(jnp.int32) for o in above))

        for o in above:

            @pl.when(both(inside(o), below_crossing))
            def _():
                copies[-o[0], -o[1], -o[2]].start()

    for copy in loads[6:]:
        copy.wait()
    index = index_ref[...]
    matrix = jnp.zeros(index.shape, jnp.float32)
    chosen = chosen_ref[...]
    table = None
    for a in range(3):
        coupling = jnp.concatenate([chosen * sten_ref[a][b : b + 1, :] for b in range(3)], axis=0)
        term = dot(coupling, widen_ref[a], HIGHEST)
        table = term if table is None else table + term
    for b in range(3):
        for km in range(9):
            matrix = jnp.where(index == km * 3 + b, table[16 * b + km : 16 * b + km + 1, :], matrix)
    high = matrix.astype(jnp.bfloat16)
    low = (matrix - high.astype(jnp.float32)).astype(jnp.bfloat16)
    for i in range(CX + 2):
        window = xp[i : i + 3].reshape(3 * PLANE, VECS)
        image = (dot(high, window) + dot(low, window)).astype(jnp.bfloat16)
        ic[i] = image[0:48]
        for k in range(4):
            iyz[k, i] = image[48 + 16 * k : 64 + 16 * k]
        icn[i] = image[112:128]
    dense = dot(regroup_ref[0], icn[1 : CX + 1].reshape(CX * 16, VECS))
    for j in range(4):
        ie[j] = dense[24 * j : 24 * j + 24].astype(jnp.bfloat16)
        iface[j] = dot(regroup_ref[1], iyz[j, 1 : CX + 1].reshape(CX * 16, VECS)).astype(jnp.bfloat16)

    def operands(o):
        xi = 0 if o[0] < 0 else CX + 1
        inner = slice(1, CX + 1)
        if o == (0, 0, 0):
            return ic[inner].reshape(CX * PLANE, VECS), xp[2 : CX + 2].reshape(CX * PLANE, VECS)
        if o[1] == 0 and o[2] == 0:
            return ic[xi], hx[side(o[0])]
        if o[0] == 0 and o[2] == 0:
            return iface[side(o[1])], hy[side(o[1])]
        if o[0] == 0 and o[1] == 0:
            return iface[2 + side(o[2])], hz[side(o[2])]
        if o[0] == 0:
            k = pair(o[1], o[2])
            return ie[k], hyz[k]
        return iyz[2 + side(o[2]), xi], hxz[pair(o[0], o[2])]

    def rows_copy(g, d, target, source):
        if g == len(GROUPS):
            src, dst = hxy, cells.at[source]
        else:
            slots = pl.ds(SLOTS[g].start, SLOTS[g].stop - SLOTS[g].start)
            src, dst = stage.at[target, slots], recv.at[source, slots]
        return pltpu.make_async_remote_copy(
            src_ref=src, dst_ref=dst, send_sem=row_send.at[g, d - 1], recv_sem=row_recv.at[g, d - 1],
            device_id=(me[0], me[1], target), device_id_type=MESH,
        )

    def arrive(o):
        @pl.when(inside(o))
        def _():
            copies[o].wait_recv()

    distances = sorted(range(1, n_z), key=lambda d: -min(d, n_z - d))

    def send(g):
        for d in distances:
            target = lax.rem(me[2] + d, n_z)

            @pl.when(negate(both(origin_line, target == 0)))
            def _():
                rows_copy(g, d, target, me[2]).start()

    def receive(g, d):
        rows_copy(g, d, lax.rem(me[2] + d, n_z), lax.rem(me[2] + n_z - d, n_z)).wait_recv()

    few = [v for x, y in CROSS for v in (iyz[side(y), (CX + 1) * side(x)], icn[(CX + 1) * side(x)])]
    few = contract(jnp.concatenate(few, axis=0), eye_ref[...]).reshape(n_z, rows, VECS).astype(jnp.bfloat16)
    stage[:, 1] = few
    for g, group in enumerate(GROUPS):
        if g == 1:
            to_the_origin(0)
        if g == 2:
            up()
            to_the_origin(1)
            for x, y in CROSS:
                arrive((x, y, 0))
            send(len(GROUPS))
            cells[me[2]] = hxy[...]
        for o in group:
            if o in copies:
                arrive(o)
        for o in group:
            left, right = operands(o)
            block = contract(left, right)
            if o != (0, 0, 0):
                block = jnp.where(inside(o), block, 0.0)
            stage[:, PLACES[ORDER.index(o)]] = block.reshape(n_z, rows, VECS).astype(jnp.bfloat16)
        send(g)

    @pl.when(both(origin_line, negate(origin)))
    def _():
        @pl.when(me[2] != 1)
        def _():
            pl.semaphore_wait(origin_ready, 1)

        for g in (0, 3, 1, 2):
            rows_copy(g, n_z - me[2], 0, me[2]).start()

    def put(o, source, value):
        out_ref[pl.ds(number(o) * n_z + source, rows, stride=27 * n_z), :] = value

    for o, k in zip(ORDER, PLACES):
        put(o, me[2], stage[me[2], k].astype(jnp.float32))
    recv[me[2], 1] = stage[me[2], 1]
    for r in NEIGHBOURS:

        @pl.when(inside((-r[0], -r[1], -r[2])))
        def _():
            copies[r].wait_send()

    for d in distances:
        receive(0, d)
        receive(len(GROUPS), d)
    few = recv[:, 1].reshape(VECS, VECS)
    from_cell = lax.broadcasted_iota(jnp.int32, (VECS, 16 * n_z), 0) // rows
    to_cell = lax.broadcasted_iota(jnp.int32, (VECS, 16 * n_z), 1) // 16
    for i, (x, y) in enumerate(CROSS):
        right = cells[:, i].reshape(n_z * 16, VECS)
        ok = inside((x, y, 0))
        for z in (-1, 0, 1):
            start = (3 * i + z + 1) * 128
            left = dot(few, choose_ref[:, start : start + 16 * n_z])
            left = jnp.where(from_cell + z == to_cell, left, 0.0).astype(jnp.bfloat16)
            block = jnp.where(ok, dot(left, right), 0.0)
            for source in range(n_z):
                put((x, y, z), source, block[source * rows : (source + 1) * rows])

    for d in reversed(distances):
        receive(1, d)
        receive(2, d)
        source = lax.rem(me[2] + n_z - d, n_z)
        for o, k in zip(ORDER, PLACES):
            put(o, source, recv[source, k].astype(jnp.float32))
    for d in distances:
        for g in range(len(GROUPS) + 1):
            rows_copy(g, d, lax.rem(me[2] + d, n_z), me[2]).wait_send()


def body(sizes, deflation, material, moduli, stencil):
    n_z = sizes[2]
    rows = VECS // n_z
    vectors = jnp.transpose(deflation, (0, 1, 3, 2, 4)).reshape(CX, PLANE, VECS)
    classes = jnp.transpose(material, (1, 2, 0)).reshape(CY * CZ, CX)
    coupling = jnp.transpose(stencil, (1, 2, 0))
    index, widen, chosen, pack, regroup, place, eye, choose = tables()
    b16 = jnp.bfloat16
    operands = (
        vectors, classes, moduli, coupling, index, widen, chosen,
        jnp.asarray(pack, b16), jnp.asarray(regroup, b16), place, jnp.asarray(eye, b16), jnp.asarray(choose, b16),
    )
    spaces = [pltpu.SMEM if k == 2 else pltpu.VMEM for k in range(len(operands))]
    out = pl.pallas_call(
        functools.partial(kernel, sizes),
        out_shape=jax.ShapeDtypeStruct((rows * 27 * n_z, VECS), jnp.float32),
        in_specs=[pl.BlockSpec(memory_space=pltpu.HBM)] * len(operands),
        out_specs=pl.BlockSpec(memory_space=pltpu.VMEM),
        scratch_shapes=[space(v.shape, v.dtype) for space, v in zip(spaces, operands)] + [
            pltpu.SemaphoreType.DMA((len(operands),)),
            pltpu.VMEM((CX + 4, PLANE, VECS), b16),
            pltpu.VMEM((5, CX, 16, VECS), b16),
            pltpu.VMEM((4, 24, VECS), b16),
            pltpu.VMEM((4, 96, VECS), b16),
            pltpu.VMEM((4, 96, VECS), b16),
            pltpu.VMEM((2, PLANE, VECS), b16),
            pltpu.VMEM((2, 96, VECS), b16),
            pltpu.VMEM((2, 96, VECS), b16),
            pltpu.VMEM((4, 24, VECS), b16),
            pltpu.VMEM((4, 16, VECS), b16),
            pltpu.VMEM((4, 16, VECS), b16),
            pltpu.VMEM((CX + 2, PLANE, VECS), b16),
            pltpu.VMEM((4, CX + 2, 16, VECS), b16),
            pltpu.VMEM((CX + 2, 16, VECS), b16),
            pltpu.VMEM((4, 24, VECS), b16),
            pltpu.VMEM((n_z, 16, rows, VECS), b16),
            pltpu.VMEM((n_z, 16, rows, VECS), b16),
            pltpu.VMEM((n_z, 4, 16, VECS), b16),
            pltpu.SemaphoreType.DMA((len(NEIGHBOURS),)),
            pltpu.SemaphoreType.DMA((len(NEIGHBOURS),)),
            pltpu.SemaphoreType.DMA((len(GROUPS) + 1, n_z - 1)),
            pltpu.SemaphoreType.DMA((len(GROUPS) + 1, n_z - 1)),
            pltpu.SemaphoreType.REGULAR,
            pltpu.SemaphoreType.REGULAR,
        ],
        compiler_params=pltpu.CompilerParams(collective_id=0, has_side_effects=True, vmem_limit_bytes=24 * 2**20),
        name="coarse",
    )(*[pltpu.with_memory_space_constraint(v, pltpu.HBM) for v in operands])
    return jnp.transpose(out.reshape(1, 1, rows, 27, n_z, VECS), (0, 1, 2, 4, 3, 5))


def solution(mesh):
    sizes = tuple(mesh.shape[name] for name in ("gx", "gy", "gz"))
    in_specs = (P("gx", "gy", "gz", None, None), P("gx", "gy", "gz"), P(), P())
    out_specs = P("gx", "gy", "gz", None, None, None)
    return jax.shard_map(
        functools.partial(body, sizes), mesh=mesh, in_specs=in_specs, out_specs=out_specs, check_vma=False
    )
```

```python
import functools

import jax
import jax.numpy as jnp
import numpy as np
from jax import lax
from jax.experimental import pallas as pl
from jax.experimental.pallas import tpu as pltpu
from jax.sharding import PartitionSpec as P

MESH = pl.DeviceIdType.MESH
HIGHEST = lax.Precision.HIGHEST
CX, CY, CZ, VECS = 8, 4, 4, 128
PLANE = CY * 3 * CZ
OFFSETS = [(i, j, k) for i in (-1, 0, 1) for j in (-1, 0, 1) for k in (-1, 0, 1)]
CROSS = [(i, j) for i in (-1, 1) for j in (-1, 1)]
NEIGHBOURS = [o for o in OFFSETS if o != (0, 0, 0) and 0 in o]
GROUPS = (
    [(0, 0, 0)],
    [o for o in NEIGHBOURS if o[1] == 0],
    [o for o in NEIGHBOURS if o[0] == 0 and o[1] != 0],
)
ORDER = [o for g in GROUPS for o in g]
SLOTS = (slice(0, 2), slice(2, 10), slice(10, 16))
PLACES = [0] + list(range(2, 16))


def number(o):
    return 9 * (o[0] + 1) + 3 * (o[1] + 1) + o[2] + 1


def side(v):
    return 1 if v > 0 else 0


def pair(v, w):
    return 2 * side(v) + side(w)


def image_rows():
    rows = [(y, z, b) for y in range(CY) for b in range(3) for z in range(CZ)]
    for y in (-1, CY):
        rows += [(y, z, b) for b in range(3) for z in range(CZ)] + [None] * 4
    for z in (-1, CZ):
        rows += [(y, z, b) for y in range(CY) for b in range(3)] + [None] * 4
    for y in (-1, CY):
        for z in (-1, CZ):
            rows += [(y, z, b) for b in range(3)] + [None]
    return rows


@functools.cache
def tables():
    rows = image_rows()
    index = np.full((128, 3 * PLANE), -1, np.int32)
    for r, row in enumerate(rows):
        if row is None:
            continue
        for p in range(3):
            for y in range(CY):
                for a in range(3):
                    for z in range(CZ):
                        oy, oz = row[0] - y, row[1] - z
                        if abs(oy) <= 1 and abs(oz) <= 1:
                            index[r, p * PLANE + y * 12 + a * 4 + z] = (3 * (oy + 1) + oz + 1) * 3 + row[2]
    widen = np.zeros((3, 27, 3 * PLANE), np.float32)
    for n in range(27):
        for y in range(CY):
            for a in range(3):
                for z in range(CZ):
                    widen[a, n, (2 - n // 9) * PLANE + y * 12 + a * 4 + z] = 1
    chosen = (np.arange(27)[None, :] % 9 == np.arange(16)[:, None]).astype(np.float32)
    pack = np.zeros((80, PLANE), np.float32)
    for r, row in enumerate(rows[48:]):
        if row is not None:
            y, z, a = row
            pack[r, (y % CY) * 12 + a * 4 + z % CZ] = 1
    regroup = np.zeros((2, 96, 128), np.float32)
    for x in range(CX):
        for j in range(4):
            for b in range(3):
                regroup[0, j * 24 + x * 3 + b, x * 16 + j * 4 + b] = 1
        for j in range(12):
            regroup[1, x * 12 + j, x * 16 + j] = 1
    place = np.zeros((PLANE, 16), np.float32)
    for y in range(CY):
        for a in range(3):
            for z in range(CZ):
                place[y * 12 + a * 4 + z, y * CZ + z] = 1
    choose = np.zeros((128, 12, 8, 16), np.float32)
    for g, (_, y) in enumerate(CROSS):
        for a in range(3):
            for z in range(CZ):
                choose[g * 32 + a * 4 + z, 3 * g + 1, :, a * 4 + z] = 1
            choose[g * 32 + 16 + pair(y, -1) * 4 + a, 3 * g, :, a * 4 + CZ - 1] = 1
            choose[g * 32 + 16 + pair(y, 1) * 4 + a, 3 * g + 2, :, a * 4] = 1
    return index, widen, chosen, pack, regroup, place, np.eye(128, dtype=np.float32), choose.reshape(128, 1536)


CROSSINGS = (3, 7)


def crossing(y):
    return functools.reduce(jnp.logical_or, [y == k for k in CROSSINGS])


def dot(a, b, precision=None):
    return jnp.dot(a, b, preferred_element_type=jnp.float32, precision=precision)


def contract(left, right):
    return lax.dot_general(left, right, (((0,), (0,)), ((), ())), preferred_element_type=jnp.float32)


def kernel(
    sizes,
    vec_in, mat_in, mod_in, sten_in, index_in, widen_in, chosen_in, pack_in, regroup_in, place_in, eye_in, choose_in,
    out_ref,
    vec_ref, mat_ref, mod_ref, sten_ref, index_ref, widen_ref, chosen_ref, pack_ref, regroup_ref, place_ref, eye_ref, choose_ref, load_sem,
    xp, pk, edge, face, iface, hx, hy, hz, hyz, hxy, hxz, ic, iyz, icn, ie, stage, recv, cells,
    halo_send, halo_recv, row_send, row_recv, ready, origin_ready,
):
    loads = [
        pltpu.make_async_copy(src, dst, load_sem.at[k])
        for k, (src, dst) in enumerate([
            (mat_in, mat_ref), (mod_in, mod_ref), (place_in, place_ref), (vec_in, vec_ref), (pack_in, pack_ref),
            (regroup_in, regroup_ref), (sten_in, sten_ref), (index_in, index_ref), (widen_in, widen_ref), (chosen_in, chosen_ref),
            (eye_in, eye_ref), (choose_in, choose_ref),
        ])
    ]
    for copy in loads:
        copy.start()
    n_z = sizes[2]
    rows = VECS // n_z
    me = (lax.axis_index("gx"), lax.axis_index("gy"), lax.axis_index("gz"))

    def at(o):
        return tuple(lax.rem(me[i] + (o[i] + sizes[i]), sizes[i]) for i in range(3))

    def inside(o):
        ok = None
        for i in range(3):
            if o[i] == 0:
                continue
            here = me[i] > 0 if o[i] < 0 else me[i] < sizes[i] - 1
            ok = here if ok is None else jnp.logical_and(ok, here)
        return ok

    both, negate = jnp.logical_and, jnp.logical_not
    origin_line = both(me[0] == 0, me[1] == 0)
    origin = both(origin_line, me[2] == 0)

    def to_origin(o):
        if max(o) > 0:
            return None
        return both(both(me[0] + o[0] == 0, me[1] + o[1] == 0), me[2] + o[2] == 0)

    def except_origin(o):
        return inside(o) if max(o) > 0 else both(inside(o), negate(to_origin(o)))

    below_crossing, above_crossing = crossing(me[1]), crossing(me[1] - 1)
    beside = [o for o in NEIGHBOURS if o[:2] != (0, 0)]
    barrier = pltpu.get_barrier_semaphore()
    expected = jnp.int32(n_z - 1) - both(origin_line, negate(origin)).astype(jnp.int32)
    for o in beside:
        awaited = both(inside(o), negate(below_crossing)) if o[1] > 0 else except_origin(o)
        expected = expected + awaited.astype(jnp.int32)
        told = inside(o) if o[1] >= 0 else both(inside(o), negate(above_crossing))

        @pl.when(both(told, negate(origin)))
        def _():
            pl.semaphore_signal(barrier, inc=1, device_id=at(o), device_id_type=MESH)

    @pl.when(negate(origin))
    def _():
        for d in range(1, n_z):
            pl.semaphore_signal(barrier, inc=1, device_id=at((0, 0, d)), device_id_type=MESH)

    @pl.when(origin)
    def _():
        pl.semaphore_wait(barrier, expected)
        for o in beside:
            if min(o) >= 0:
                pl.semaphore_signal(origin_ready, inc=1, device_id=at(o), device_id_type=MESH)
        for d in range(1, n_z):
            pl.semaphore_signal(origin_ready, inc=1, device_id=at((0, 0, d)), device_id_type=MESH)

    for copy in loads[:6]:
        copy.wait()
    mat = mat_ref[...]
    value = jnp.zeros(mat.shape, jnp.float32)
    for c in range(16):
        value = jnp.where(mat == c, mod_ref[c], value)
    root = jnp.sqrt(value)
    wide = jnp.concatenate([jnp.broadcast_to(root[:, x : x + 1], (16, VECS)) for x in range(CX)], axis=1)
    scale = dot(place_ref[...], wide, HIGHEST)
    empty = jnp.zeros((PLANE, VECS), jnp.bfloat16)
    for i in (0, 1, CX + 2, CX + 3):
        xp[i] = empty
    for x in range(CX):
        plane = (vec_ref[x].astype(jnp.float32) * scale[:, x * VECS : (x + 1) * VECS]).astype(jnp.bfloat16)
        xp[2 + x] = plane
        packed = dot(pack_ref[...], plane)
        for k in range(5):
            pk[k, x] = packed[16 * k : 16 * k + 16].astype(jnp.bfloat16)
    dense = dot(regroup_ref[0], pk[4].reshape(CX * 16, VECS))
    for j in range(4):
        edge[j] = dense[24 * j : 24 * j + 24].astype(jnp.bfloat16)
        face[j] = dot(regroup_ref[1], pk[j].reshape(CX * 16, VECS)).astype(jnp.bfloat16)

    def halo(r):
        xi = CX - 1 if r[0] < 0 else 0
        if r[1] == 0 and r[2] == 0:
            return xp.at[2 + xi], hx.at[side(r[0])]
        if r[0] == 0 and r[2] == 0:
            return face.at[side(r[1])], hy.at[side(r[1])]
        if r[0] == 0 and r[1] == 0:
            return face.at[2 + side(r[2])], hz.at[side(r[2])]
        if r[0] == 0:
            return edge.at[pair(r[1], r[2])], hyz.at[pair(r[1], r[2])]
        if r[2] == 0:
            return pk.at[side(r[1]), xi], hxy.at[pair(r[0], r[1])]
        return pk.at[2 + side(r[2]), xi], hxz.at[pair(r[0], r[2])]

    copies = {}
    for r in sorted(NEIGHBOURS, key=lambda r: (r[1] == 0, -abs(r[0]) - abs(r[2]))):
        src, dst = halo(r)
        k = NEIGHBOURS.index(r)
        copies[r] = pltpu.make_async_remote_copy(
            src_ref=src, dst_ref=dst, send_sem=halo_send.at[k], recv_sem=halo_recv.at[k],
            device_id=at((-r[0], -r[1], -r[2])), device_id_type=MESH,
        )

    @pl.when(origin)
    def _():
        for r in NEIGHBOURS:
            if max(r) <= 0:
                copies[r].start()

    @pl.when(negate(origin))
    def _():
        pl.semaphore_wait(barrier, expected)

    for o in beside:
        if o[1] < 0:

            @pl.when(both(inside(o), above_crossing))
            def _():
                pl.semaphore_signal(ready, inc=1, device_id=at(o), device_id_type=MESH)

    for r in NEIGHBOURS:
        o = (-r[0], -r[1], -r[2])
        at_once = both(inside(o), negate(below_crossing)) if o[1] > 0 else except_origin(o)

        @pl.when(both(at_once, negate(origin)))
        def _():
            copies[r].start()

    def to_the_origin(level):
        for r in NEIGHBOURS:
            if min(r) >= 0 and r[1] == level:

                @pl.when(to_origin((-r[0], -r[1], -r[2])))
                def _():
                    pl.semaphore_wait(origin_ready, 1)
                    copies[r].start()

    def up():
        above = [o for o in beside if o[1] > 0]

        @pl.when(below_crossing)
        def _():
            pl.semaphore_wait(ready, sum(inside(o).astype(jnp.int32) for o in above))

        for o in above:

            @pl.when(both(inside(o), below_crossing))
            def _():
                copies[-o[0], -o[1], -o[2]].start()

    for copy in loads[6:]:
        copy.wait()
    index = index_ref[...]
    matrix = jnp.zeros(index.shape, jnp.float32)
    chosen = chosen_ref[...]
    table = None
    for a in range(3):
        coupling = jnp.concatenate([chosen * sten_ref[a][b : b + 1, :] for b in range(3)], axis=0)
        term = dot(coupling, widen_ref[a], HIGHEST)
        table = term if table is None else table + term
    for b in range(3):
        for km in range(9):
            matrix = jnp.where(index == km * 3 + b, table[16 * b + km : 16 * b + km + 1, :], matrix)
    high = matrix.astype(jnp.bfloat16)
    low = (matrix - high.astype(jnp.float32)).astype(jnp.bfloat16)
    for i in range(CX + 2):
        window = xp[i : i + 3].reshape(3 * PLANE, VECS)
        image = (dot(high, window) + dot(low, window)).astype(jnp.bfloat16)
        ic[i] = image[0:48]
        for k in range(4):
            iyz[k, i] = image[48 + 16 * k : 64 + 16 * k]
        icn[i] = image[112:128]
    def operands(o):
        xi = 0 if o[0] < 0 else CX + 1
        inner = slice(1, CX + 1)
        if o == (0, 0, 0):
            return ic[inner].reshape(CX * PLANE, VECS), xp[2 : CX + 2].reshape(CX * PLANE, VECS)
        if o[1] == 0 and o[2] == 0:
            return ic[xi], hx[side(o[0])]
        if o[0] == 0 and o[2] == 0:
            return iface[side(o[1])], hy[side(o[1])]
        if o[0] == 0 and o[1] == 0:
            return iface[2 + side(o[2])], hz[side(o[2])]
        if o[0] == 0:
            k = pair(o[1], o[2])
            return ie[k], hyz[k]
        return iyz[2 + side(o[2]), xi], hxz[pair(o[0], o[2])]

    def rows_copy(g, d, target, source):
        if g == len(GROUPS):
            src, dst = hxy, cells.at[source]
        else:
            slots = pl.ds(SLOTS[g].start, SLOTS[g].stop - SLOTS[g].start)
            src, dst = stage.at[target, slots], recv.at[source, slots]
        return pltpu.make_async_remote_copy(
            src_ref=src, dst_ref=dst, send_sem=row_send.at[g, d - 1], recv_sem=row_recv.at[g, d - 1],
            device_id=(me[0], me[1], target), device_id_type=MESH,
        )

    def arrive(o):
        @pl.when(inside(o))
        def _():
            copies[o].wait_recv()

    distances = sorted(range(1, n_z), key=lambda d: -min(d, n_z - d))

    def send(g):
        for d in distances:
            target = lax.rem(me[2] + d, n_z)

            @pl.when(negate(both(origin_line, target == 0)))
            def _():
                rows_copy(g, d, target, me[2]).start()

    def receive(g, d):
        rows_copy(g, d, lax.rem(me[2] + d, n_z), lax.rem(me[2] + n_z - d, n_z)).wait_recv()

    few = [v for x, y in CROSS for v in (iyz[side(y), (CX + 1) * side(x)], icn[(CX + 1) * side(x)])]
    few = contract(jnp.concatenate(few, axis=0), eye_ref[...]).reshape(n_z, rows, VECS).astype(jnp.bfloat16)
    stage[:, 1] = few
    for g, group in enumerate(GROUPS):
        if g == 1:
            dense = dot(regroup_ref[0], icn[1 : CX + 1].reshape(CX * 16, VECS))
            for j in range(4):
                ie[j] = dense[24 * j : 24 * j + 24].astype(jnp.bfloat16)
                iface[j] = dot(regroup_ref[1], iyz[j, 1 : CX + 1].reshape(CX * 16, VECS)).astype(jnp.bfloat16)
            to_the_origin(0)
        if g == 2:
            up()
            to_the_origin(1)
            for x, y in CROSS:
                arrive((x, y, 0))
            send(len(GROUPS))
            cells[me[2]] = hxy[...]
        for o in group:
            if o in copies:
                arrive(o)
        for o in group:
            left, right = operands(o)
            block = contract(left, right)
            if o != (0, 0, 0):
                block = jnp.where(inside(o), block, 0.0)
            stage[:, PLACES[ORDER.index(o)]] = block.reshape(n_z, rows, VECS).astype(jnp.bfloat16)
        send(g)

    @pl.when(both(origin_line, negate(origin)))
    def _():
        @pl.when(me[2] != 1)
        def _():
            pl.semaphore_wait(origin_ready, 1)

        for g in (0, 3, 1, 2):
            rows_copy(g, n_z - me[2], 0, me[2]).start()

    def put(o, source, value):
        out_ref[pl.ds(number(o) * n_z + source, rows, stride=27 * n_z), :] = value

    for o, k in zip(ORDER, PLACES):
        put(o, me[2], stage[me[2], k].astype(jnp.float32))
    recv[me[2], 1] = stage[me[2], 1]
    for r in NEIGHBOURS:

        @pl.when(inside((-r[0], -r[1], -r[2])))
        def _():
            copies[r].wait_send()

    for d in distances:
        receive(0, d)
        receive(len(GROUPS), d)
    few = recv[:, 1].reshape(VECS, VECS)
    from_cell = lax.broadcasted_iota(jnp.int32, (VECS, 16 * n_z), 0) // rows
    to_cell = lax.broadcasted_iota(jnp.int32, (VECS, 16 * n_z), 1) // 16
    for i, (x, y) in enumerate(CROSS):
        right = cells[:, i].reshape(n_z * 16, VECS)
        ok = inside((x, y, 0))
        for z in (-1, 0, 1):
            start = (3 * i + z + 1) * 128
            left = dot(few, choose_ref[:, start : start + 16 * n_z])
            left = jnp.where(from_cell + z == to_cell, left, 0.0).astype(jnp.bfloat16)
            block = jnp.where(ok, dot(left, right), 0.0)
            for source in range(n_z):
                put((x, y, z), source, block[source * rows : (source + 1) * rows])

    for d in reversed(distances):
        receive(1, d)
        receive(2, d)
        source = lax.rem(me[2] + n_z - d, n_z)
        for o, k in zip(ORDER, PLACES):
            put(o, source, recv[source, k].astype(jnp.float32))
    for d in distances:
        for g in range(len(GROUPS) + 1):
            rows_copy(g, d, lax.rem(me[2] + d, n_z), me[2]).wait_send()


def body(sizes, deflation, material, moduli, stencil):
    n_z = sizes[2]
    rows = VECS // n_z
    vectors = jnp.transpose(deflation, (0, 1, 3, 2, 4)).reshape(CX, PLANE, VECS)
    classes = jnp.transpose(material, (1, 2, 0)).reshape(CY * CZ, CX)
    coupling = jnp.transpose(stencil, (1, 2, 0))
    index, widen, chosen, pack, regroup, place, eye, choose = tables()
    b16 = jnp.bfloat16
    operands = (
        vectors, classes, moduli, coupling, index, widen, chosen,
        jnp.asarray(pack, b16), jnp.asarray(regroup, b16), place, jnp.asarray(eye, b16), jnp.asarray(choose, b16),
    )
    spaces = [pltpu.SMEM if k == 2 else pltpu.VMEM for k in range(len(operands))]
    out = pl.pallas_call(
        functools.partial(kernel, sizes),
        out_shape=jax.ShapeDtypeStruct((rows * 27 * n_z, VECS), jnp.float32),
        in_specs=[pl.BlockSpec(memory_space=pltpu.HBM)] * len(operands),
        out_specs=pl.BlockSpec(memory_space=pltpu.VMEM),
        scratch_shapes=[space(v.shape, v.dtype) for space, v in zip(spaces, operands)] + [
            pltpu.SemaphoreType.DMA((len(operands),)),
            pltpu.VMEM((CX + 4, PLANE, VECS), b16),
            pltpu.VMEM((5, CX, 16, VECS), b16),
            pltpu.VMEM((4, 24, VECS), b16),
            pltpu.VMEM((4, 96, VECS), b16),
            pltpu.VMEM((4, 96, VECS), b16),
            pltpu.VMEM((2, PLANE, VECS), b16),
            pltpu.VMEM((2, 96, VECS), b16),
            pltpu.VMEM((2, 96, VECS), b16),
            pltpu.VMEM((4, 24, VECS), b16),
            pltpu.VMEM((4, 16, VECS), b16),
            pltpu.VMEM((4, 16, VECS), b16),
            pltpu.VMEM((CX + 2, PLANE, VECS), b16),
            pltpu.VMEM((4, CX + 2, 16, VECS), b16),
            pltpu.VMEM((CX + 2, 16, VECS), b16),
            pltpu.VMEM((4, 24, VECS), b16),
            pltpu.VMEM((n_z, 16, rows, VECS), b16),
            pltpu.VMEM((n_z, 16, rows, VECS), b16),
            pltpu.VMEM((n_z, 4, 16, VECS), b16),
            pltpu.SemaphoreType.DMA((len(NEIGHBOURS),)),
            pltpu.SemaphoreType.DMA((len(NEIGHBOURS),)),
            pltpu.SemaphoreType.DMA((len(GROUPS) + 1, n_z - 1)),
            pltpu.SemaphoreType.DMA((len(GROUPS) + 1, n_z - 1)),
            pltpu.SemaphoreType.REGULAR,
            pltpu.SemaphoreType.REGULAR,
        ],
        compiler_params=pltpu.CompilerParams(collective_id=0, has_side_effects=True, vmem_limit_bytes=24 * 2**20),
        name="coarse",
    )(*[pltpu.with_memory_space_constraint(v, pltpu.HBM) for v in operands])
    return jnp.transpose(out.reshape(1, 1, rows, 27, n_z, VECS), (0, 1, 2, 4, 3, 5))


def solution(mesh):
    sizes = tuple(mesh.shape[name] for name in ("gx", "gy", "gz"))
    in_specs = (P("gx", "gy", "gz", None, None), P("gx", "gy", "gz"), P(), P())
    out_specs = P("gx", "gy", "gz", None, None, None)
    return jax.shard_map(
        functools.partial(body, sizes), mesh=mesh, in_specs=in_specs, out_specs=out_specs, check_vma=False
    )
```
